256 devices in a mesh: tile: 64 (over y, x_hi, z), layer: 4 (over x_lo, core).
Axes of the slice: x: 4 (x_hi: 2, x_lo: 2; x = x_hi * 2 + x_lo), y: 4, z: 8, core: 2. Of those that a mesh axis runs over, the one named last changes fastest.
Arguments:
- forcing: float32 [16, 16, 512, 512], P('layer', None, 'tile'), may hold values from -6 to 6
- vert_coupling: float32 [16, 512, 512], P(None, 'tile', 'layer'), may hold values from 0.25 to 4
- horiz_coupling: float32 [512, 512], P('tile'), may hold values from 0.25 to 2
- basal_velocity: float32 [512, 512], P('tile', 'layer'), may hold values from 0.5 to 10
- group_label: int32 [512, 512], P('tile', 'layer'), may hold values from 0 to 511
- ice_mask: int32 [512, 512], P('tile', 'layer'), may hold values 0 or 1
Outputs:
- adjoint: float32 [16, 16, 512, 512], P('layer', None, 'tile')
- sensitivity: float32 [16, 512], replicated
The draws below stay inside these ranges and needn't reach their ends.
All inputs are finite; a program needn't handle non-finite values. No bound on the sum of `ice_mask` on one device may be relied on, other than what follows from the above.
Results may differ from the reference program's by a relative error of at most 0.0001.
Values sent between devices are 32-bit elements; how exact they have to be, the bound alone decides.
A program may use at most 64 MiB of HBM per device.

```python
import math
import jax
import jax.numpy as jnp
from jax import lax

F = 16
GROUPS = 512
NL = 16
SWEEPS = 2
RX = 512
NY = 512


def touch_ends(array, own_key, low, high):
    longest = array.shape.index(max(array.shape))
    spots = []
    for shift in (0, 1):
        where = [jax.random.randint(jax.random.fold_in(own_key, axis), (), 0, length) for axis, length in enumerate(array.shape)]
        where[longest] = (where[longest] + shift) % array.shape[longest]
        spots.append(tuple(where))
    return array.at[spots[0]].set(low).at[spots[1]].set(high)


def steps_of(rng, shape, cuts, low, high):
    loudness, own = 1.0, jax.random.fold_in(rng, 6)
    for axis_at, blocks in cuts:
        steps = jnp.exp(jax.random.uniform(jax.random.fold_in(own, axis_at), (blocks,), jnp.float32, low / len(cuts), high / len(cuts)))
        loudness = loudness * jnp.repeat(steps, shape[axis_at] // blocks).reshape([-1 if axis == axis_at else 1 for axis in range(len(shape))])
    return loudness


def normal_values(key, dims, width, most, pieces=(), kind=jnp.bfloat16):
    entries = jax.random.normal(key, dims, jnp.float32) * width
    if len(pieces) > 0:
        entries = steps_of(key, dims, pieces, -0.22, 0.18) * entries
    return jnp.clip(entries, min=-most, max=most).astype(kind)


def setup_inputs(seed: int = 0) -> dict:
    arg_keys = jax.random.split(jax.random.key(seed), 7)
    return {
        "forcing": normal_values(arg_keys[0], (NL, F, NY, RX), 1.0, 6.0, ((0, 4), (2, 64)), jnp.float32),
        "vert_coupling": jnp.clip(jnp.exp(math.log(4.0) - 2.7725887 * jax.random.uniform(arg_keys[1], (NL, NY, RX), jnp.float32) ** steps_of(arg_keys[1], (NL, NY, RX), ((1, 64), (2, 4)), -0.2, 0.2)), 0.25, 4.0),
        "horiz_coupling": jnp.clip(jnp.exp(math.log(2.0) - 2.0794415 * jax.random.uniform(arg_keys[2], (NY, RX), jnp.float32) ** steps_of(arg_keys[2], (NY, RX), ((0, 64),), -0.2, 0.2)), 0.25, 2.0),
        "basal_velocity": jnp.clip(jnp.exp(math.log(10.0) - 2.9957323 * jax.random.uniform(arg_keys[3], (NY, RX), jnp.float32) ** steps_of(arg_keys[3], (NY, RX), ((0, 64), (1, 4)), -0.2, 0.2)), 0.5, 10.0),
        "group_label": touch_ends(jax.random.randint(arg_keys[4], (NY, RX), 0, GROUPS), jax.random.fold_in(arg_keys[4], 1), 0, GROUPS - 1).astype(jnp.int32),
        "ice_mask": touch_ends((jax.random.randint(arg_keys[5], (NY, RX), 0, 4) < 3).astype(jnp.int32), jax.random.fold_in(arg_keys[5], 1), 0, 1),
    }


def column_solve(rhs, sub_diag, full_diag, super_diag):
    def forward(running, layer_in):
        c_prime, d_prime = running
        sub_k, diag_k, super_k, rhs_k = layer_in
        pivot = diag_k - sub_k * c_prime
        c_next = super_k / pivot
        d_next = (rhs_k - sub_k * d_prime) / pivot
        return (c_next, d_next), (c_next, d_next)

    start = (jnp.zeros_like(full_diag[0]), jnp.zeros_like(rhs[0]))
    _, (c_all, d_all) = lax.scan(forward, start, (sub_diag, full_diag, super_diag, rhs))

    def backward(solved_up, layer_in):
        c_here, d_here = layer_in
        solved = d_here - c_here * solved_up
        return solved, solved

    _, result = lax.scan(backward, jnp.zeros_like(rhs[0]), (c_all, d_all), reverse=True)
    return result


def vertical_apply(field, sub_diag, vert_diag, super_diag):
    zero_layer = jnp.zeros_like(field[:1])
    below = jnp.concatenate([zero_layer, field[:-1]], axis=0)
    above = jnp.concatenate([field[1:], zero_layer], axis=0)
    return vert_diag * field + sub_diag * below + super_diag * above


def reference(forcing, vert_coupling, horiz_coupling, basal_velocity, group_label, ice_mask):
    zero_layer = jnp.zeros_like(vert_coupling[:1])
    coupling_next = jnp.concatenate([vert_coupling[1:], zero_layer], axis=0)
    sub_diag = jnp.concatenate([zero_layer, -vert_coupling[1:]], axis=0)
    super_diag = -coupling_next
    vert_diag = vert_coupling + coupling_next
    full_diag = vert_diag + 4.0 * horiz_coupling

    def horizontal(field):
        padded = jnp.pad(field, ((0, 0), (1, 1), (1, 1)))
        return horiz_coupling * (4.0 * field - padded[:, :-2, 1:-1] - padded[:, 2:, 1:-1]
                                 - padded[:, 1:-1, :-2] - padded[:, 1:-1, 2:])

    def solve_single(forcing_one):
        adjoint_one = column_solve(forcing_one, sub_diag, full_diag, super_diag)
        for sweep in range(SWEEPS - 1):
            residual = forcing_one - (horizontal(adjoint_one) + vertical_apply(adjoint_one, sub_diag, vert_diag, super_diag))
            adjoint_one = adjoint_one + column_solve(residual, sub_diag, full_diag, super_diag)
        return adjoint_one

    adjoint_all = lax.map(solve_single, jnp.moveaxis(forcing, 1, 0))
    adjoint = jnp.moveaxis(adjoint_all, 0, 1)
    weight = vert_coupling[0] * basal_velocity * ice_mask.astype(jnp.float32)
    weighted = (adjoint_all[:, 0] * weight).reshape(F, NY * RX)
    totals = jax.ops.segment_sum(weighted.T, group_label.reshape(-1).astype(jnp.int32), num_segments=GROUPS)
    sensitivity = -totals.T * ((NY * RX / GROUPS) ** -0.5)
    return adjoint, sensitivity
```

```python
import functools

import jax
import jax.numpy as jnp
from jax import lax
from jax.experimental import pallas as pl
from jax.experimental.pallas import tpu as pltpu
from jax.sharding import PartitionSpec as P

GROUPS = 512
LANES = 128
MESH = pl.DeviceIdType.MESH
F32 = jnp.float32


def kernel(
    tiles, scale,
    forc, vert, horiz, basal, label, mask,
    out, sens,
    vv, hh, bb, ll, mm, pack, vb, fb, db, ip, gg, cp, den, cz, mr, mr2,
    et, eb, ht, hb, zz, oh, part, s1, s2, s3, res,
    lsem, fsem, csem_s, csem_r, xsem_s, xsem_r, m1_s, m1_r, m2_s, m2_r,
    up_s, up_r, dn_s, dn_r, o_s, o_r, ol, r_s, r_r, g_s, g_r,
):
    nf = fb.shape[1]
    nh = fb.shape[0]
    half = nh // 2
    t = lax.axis_index("tile")
    l = lax.axis_index("layer")
    p = l // 2
    c = l - 2 * p
    g2 = min(4, tiles // 4)
    g3 = tiles // (4 * g2)
    zl = t % 4
    m = (t // 4) % g2
    y = t // (4 * g2)
    partner = 2 * p + 1 - c
    cross = 2 * (1 - p) + c
    diag = 2 * (1 - p) + 1 - c

    def remote(src, dst, ssem, rsem, tile, layer):
        return pltpu.make_async_remote_copy(
            src_ref=src, dst_ref=dst, send_sem=ssem, recv_sem=rsem,
            device_id=(tile, layer), device_id_type=MESH,
        )

    local = [
        pltpu.make_async_copy(vert, vv, lsem.at[0]),
        pltpu.make_async_copy(horiz, hh, lsem.at[1]),
        pltpu.make_async_copy(basal, bb, lsem.at[2]),
        pltpu.make_async_copy(label, ll, lsem.at[3]),
        pltpu.make_async_copy(mask, mm, lsem.at[4]),
        pltpu.make_async_copy(
            forc.at[:, pl.ds(c * nf, nf)], fb.at[pl.ds(c * half, half)], lsem.at[5]
        ),
    ]
    for copy in local:
        copy.start()

    barrier = pltpu.get_barrier_semaphore()

    def greet(tile, layer):
        pl.semaphore_signal(barrier, inc=1, device_id=(tile, layer), device_id_type=MESH)

    count = 15
    for dz in range(4):
        for dl in range(4):
            if dz or dl:
                greet(t - zl + (zl + dz) % 4, (l + dl) % 4)
    for dm in range(1, g2):
        greet(t + 4 * ((m + dm) % g2 - m), l)
        count += 1
    for dy in range(1, g3):
        greet(t + 4 * g2 * ((y + dy) % g3 - y), l)
        count += 1
    first = jnp.logical_and(zl == 0, t > 0)
    last = jnp.logical_and(zl == 3, t < tiles - 1)

    @pl.when(first)
    def _():
        greet(t - 1, l)

    @pl.when(last)
    def _():
        greet(t + 1, l)

    for copy in local[:5]:
        copy.wait()
    for q in range(2):
        pack[q, 0:9] = vv[7 * q : 7 * q + 9]
        pack[q, 9] = vv[0] * bb[...] * mm[...].astype(F32)
        pack[q, 10] = ll[...].astype(F32)
    vb[l] = pack[p]

    pl.semaphore_wait(barrier, count + first.astype(jnp.int32) + last.astype(jnp.int32))

    coefs = [
        remote(pack.at[1 - p], vb.at[l], csem_s.at[0], csem_r.at[0], t, cross),
        remote(pack.at[1 - p], vb.at[l], csem_s.at[1], csem_r.at[1], t, diag),
        remote(pack.at[p], vb.at[l], csem_s.at[2], csem_r.at[2], t, partner),
    ]
    for copy in coefs:
        copy.start()
    swap = remote(
        forc.at[:, pl.ds((1 - c) * nf, nf)], fb.at[pl.ds(c * half, half)],
        fsem.at[0], fsem.at[1], t, partner,
    )
    swap.start()

    @pl.when(t == 0)
    def _():
        ht[...] = jnp.zeros_like(ht)

    @pl.when(t == tiles - 1)
    def _():
        hb[...] = jnp.zeros_like(hb)

    for copy in coefs:
        copy.wait_recv()

    blocks = hh.shape[1] // LANES
    for q in range(blocks):
        cols = slice(q * LANES, (q + 1) * LANES)
        h4 = 4.0 * hh[:, cols]
        outer = vb[q, 9 * p] * (1 - p).astype(F32)
        prev = None
        for i in range(nh):
            inner = vb[q, (i + 1) + p * (9 - 2 * (i + 1))]
            pivot = outer + inner + h4
            if prev is not None:
                pivot = pivot - outer * prev
            inverse = 1.0 / pivot
            prev = inner * inverse
            ip[i, :, cols] = inverse
            gg[i, :, cols] = outer * inverse
            cp[i, :, cols] = prev
            outer = inner
    middle = remote(cp.at[nh - 1], cz, xsem_s, xsem_r, t, cross)
    middle.start()

    def at(i):
        return i + p * (nh - 1 - 2 * i)

    local[5].wait()
    swap.wait_recv()

    def mid1(f):
        return remote(fb.at[at(nh - 1), f], mr.at[f], m1_s.at[f], m1_r.at[f], t, cross)

    def mid2(f):
        return remote(db.at[nh - 1, f], mr2.at[f], m2_s.at[f], m2_r.at[f], t, cross)

    def up(f):
        return remote(et.at[f], hb.at[f], up_s.at[f], up_r.at[f], t - 1, l)

    def down(f):
        return remote(eb.at[f], ht.at[f], dn_s.at[f], dn_r.at[f], t + 1, l)

    def forward1(f, carry):
        d = None
        for i in range(nh):
            d_new = fb[at(i), f] * ip[i]
            d = d_new if d is None else d_new + gg[i] * d
            fb[at(i), f] = d
        mid1(f).start()
        return carry

    lax.fori_loop(0, nf, forward1, 0)

    for r in range(hh.shape[0]):
        row = jnp.concatenate([vb[q, 10, r : r + 1, :] for q in range(blocks)], axis=1)
        low = row.astype(jnp.int32) % LANES
        groups = lax.broadcasted_iota(jnp.int32, (LANES, blocks * LANES), 0)
        oh[r] = (groups == low).astype(F32).astype(jnp.bfloat16)

    middle.wait_recv()
    den[...] = 1.0 / (1.0 - cp[nh - 1] * cz[...])

    def backward1(f, carry):
        mid1(f).wait()
        x = None
        for i in range(nh - 1, -1, -1):
            if x is None:
                x = (fb[at(i), f] + cp[i] * mr[f]) * den[...]
            else:
                x = fb[at(i), f] + cp[i] * x
            fb[at(i), f] = x
            et[f, i : i + 1, :] = x[0:1, :]
            eb[f, i : i + 1, :] = x[7:8, :]

        @pl.when(t > 0)
        def _():
            up(f).start()

        @pl.when(t < tiles - 1)
        def _():
            down(f).start()

        return carry

    lax.fori_loop(0, nf, backward1, 0)

    shape = (hh.shape[0], hh.shape[1])
    rows = lax.broadcasted_iota(jnp.int32, shape, 0)
    columns = lax.broadcasted_iota(jnp.int32, shape, 1)

    def forward2(f, carry):
        @pl.when(t > 0)
        def _():
            down(f).wait_recv()

        @pl.when(t < tiles - 1)
        def _():
            up(f).wait_recv()

        d = None
        for i in range(nh):
            x = fb[at(i), f]
            above = jnp.where(rows == 0, ht[f, i : i + 1, :], pltpu.roll(x, 1, axis=0))
            below = jnp.where(rows == 7, hb[f, i : i + 1, :], pltpu.roll(x, 7, axis=0))
            left = jnp.where(columns == 0, 0.0, pltpu.roll(x, 1, axis=1))
            right = jnp.where(
                columns == shape[1] - 1, 0.0, pltpu.roll(x, shape[1] - 1, axis=1)
            )
            residual = hh[...] * ((above + below) + (left + right))
            d_new = residual * ip[i]
            d = d_new if d is None else d_new + gg[i] * d
            db[i, f] = d
        mid2(f).start()
        return carry

    lax.fori_loop(0, nf, forward2, 0)

    def give(f):
        return remote(
            fb.at[pl.ds((1 - c) * half, half), f], out.at[:, c * nf + f],
            o_s.at[f], o_r.at[f], t, partner,
        )

    def keep(f):
        return pltpu.make_async_copy(
            fb.at[pl.ds(c * half, half), f], out.at[:, c * nf + f], ol.at[f]
        )

    def backward2(f, carry):
        mid2(f).wait()
        y2 = None
        for i in range(nh - 1, -1, -1):
            if y2 is None:
                y2 = (db[i, f] + cp[i] * mr2[f]) * den[...]
            else:
                y2 = db[i, f] + cp[i] * y2
            fb[at(i), f] = fb[at(i), f] + y2
        give(f).start()
        keep(f).start()
        return carry

    lax.fori_loop(0, nf, backward2, 0)

    def gather_copy(dz, layer):
        return remote(
            res.at[c, zl], res.at[c, zl], g_s.at[dz, layer], g_r.at[c, dz],
            t - zl + (zl + dz) % 4, layer,
        )

    @pl.when(p == 0)
    def _():
        weight = jnp.concatenate([vb[q, 9] for q in range(blocks)], axis=1)
        for f in range(nf):
            weighted = fb[0, f] * weight
            for r in range(hh.shape[0]):
                zz[r, f : f + 1, :] = weighted[r : r + 1, :]
        total = jnp.zeros((12 * nf, LANES), F32)
        for r in range(hh.shape[0]):
            row = jnp.concatenate([vb[q, 10, r : r + 1, :] for q in range(blocks)], axis=1)
            high = row.astype(jnp.int32) // LANES
            z = zz[r]
            spread = jnp.concatenate([jnp.where(high == g, z, 0.0) for g in range(4)], axis=0)
            a0 = spread.astype(jnp.bfloat16)
            rest = spread - a0.astype(F32)
            a1 = rest.astype(jnp.bfloat16)
            a2 = (rest - a1.astype(F32)).astype(jnp.bfloat16)
            total += lax.dot_general(
                jnp.concatenate([a0, a1, a2], axis=0), oh[r],
                (((1,), (1,)), ((), ())), preferred_element_type=F32,
            )
        n = 4 * nf
        sums = (total[2 * n :] + total[n : 2 * n]) + total[:n]
        for g in range(4):
            part[g] = sums[g * nf : (g + 1) * nf]

        s1[zl] = part[zl]
        stage = []
        for d in range(1, 4):
            there = (zl + d) % 4
            stage.append(
                remote(part.at[there], s1.at[zl], r_s.at[0, d - 1], r_r.at[0, d - 1],
                       t - zl + there, l)
            )
        for copy in stage:
            copy.start()
        for copy in stage:
            copy.wait()
        value = (s1[0] + s1[1]) + (s1[2] + s1[3])
        for number, size, mine, stride, buffer in ((1, g2, m, 4, s2), (2, g3, y, 4 * g2, s3)):
            if size == 1:
                continue
            buffer[mine] = value
            stage = [
                remote(buffer.at[mine], buffer.at[mine], r_s.at[number, d - 1],
                       r_r.at[number, d - 1], t + stride * ((mine + d) % size - mine), l)
                for d in range(1, size)
            ]
            for copy in stage:
                copy.start()
            for copy in stage:
                copy.wait()
            value = buffer[0]
            for k in range(1, size):
                value = value + buffer[k]
        res[c, zl] = value * scale
        for dz in range(4):
            for layer in range(4):
                if dz:
                    gather_copy(dz, layer).start()
                else:
                    @pl.when(layer != l)
                    def _():
                        gather_copy(dz, layer).start()

    for dz in range(4):
        for core in range(2):
            source = (zl - dz + 4) % 4
            arrival = remote(
                res.at[core, source], res.at[core, source], g_s.at[0, 0], g_r.at[core, dz], t, partner
            )
            if dz:
                arrival.wait_recv()
            else:
                @pl.when(l != core)
                def _():
                    arrival.wait_recv()
    for core in range(2):
        for g in range(4):
            sens[core * nf : (core + 1) * nf, g * LANES : (g + 1) * LANES] = res[core, g]

    for copy in coefs:
        copy.wait_send()
    swap.wait_send()
    middle.wait_send()

    def drain(f, carry):
        @pl.when(t > 0)
        def _():
            up(f).wait_send()

        @pl.when(t < tiles - 1)
        def _():
            down(f).wait_send()

        keep(f).wait()
        give(f).wait()
        return carry

    lax.fori_loop(0, nf, drain, 0)

    @pl.when(p == 0)
    def _():
        for dz in range(4):
            for layer in range(4):
                if dz:
                    gather_copy(dz, layer).wait_send()
                else:
                    @pl.when(layer != l)
                    def _():
                        gather_copy(dz, layer).wait_send()


def shards(forcing, vert_coupling, horiz_coupling, basal_velocity, group_label, ice_mask):
    tiles = lax.axis_size("tile")
    layers, functionals, rows, width = forcing.shape
    nf = functionals // 2
    nh = 2 * layers
    scale = -((tiles * rows * width / GROUPS) ** (-0.5))
    dma = pltpu.SemaphoreType.DMA
    vmem = pltpu.VMEM
    any_spec = pl.BlockSpec(memory_space=pl.ANY)
    field = (nh, nf, rows, width)
    per_f = (nf, rows, width)
    flat = (rows, width)
    scratch = [
        vmem(vert_coupling.shape, F32), vmem(flat, F32), vmem((rows, LANES), F32),
        vmem((rows, LANES), jnp.int32), vmem((rows, LANES), jnp.int32),
        vmem((2, 11, rows, LANES), F32), vmem((4, 11, rows, LANES), F32),
        vmem(field, F32), vmem(field, F32),
        vmem((nh,) + flat, F32), vmem((nh,) + flat, F32), vmem((nh,) + flat, F32),
        vmem(flat, F32), vmem(flat, F32), vmem(per_f, F32), vmem(per_f, F32),
        vmem((nf, nh, width), F32), vmem((nf, nh, width), F32),
        vmem((nf, nh, width), F32), vmem((nf, nh, width), F32),
        vmem((rows, nf, width), F32), vmem((rows, LANES, width), jnp.bfloat16),
        vmem((4, nf, LANES), F32), vmem((4, nf, LANES), F32), vmem((4, nf, LANES), F32),
        vmem((4, nf, LANES), F32), vmem((2, 4, nf, LANES), F32),
        dma((6,)), dma((2,)), dma((3,)), dma((3,)), dma, dma,
        dma((nf,)), dma((nf,)), dma((nf,)), dma((nf,)),
        dma((nf,)), dma((nf,)), dma((nf,)), dma((nf,)),
        dma((nf,)), dma((nf,)), dma((nf,)),
        dma((3, 3)), dma((3, 3)), dma((4, 4)), dma((2, 4)),
    ]
    return pl.pallas_call(
        functools.partial(kernel, tiles, scale),
        out_shape=(
            jax.ShapeDtypeStruct(forcing.shape, F32),
            jax.ShapeDtypeStruct((functionals, GROUPS), F32),
        ),
        in_specs=[any_spec] * 6,
        out_specs=(any_spec, pl.BlockSpec(memory_space=pltpu.VMEM)),
        scratch_shapes=scratch,
        compiler_params=pltpu.CompilerParams(
            collective_id=0, has_side_effects=True, vmem_limit_bytes=32 * 1024 * 1024
        ),
        name="sweeps",
    )(forcing, vert_coupling, horiz_coupling, basal_velocity, group_label, ice_mask)


def solution(mesh):
    in_specs = (
        P("layer", None, "tile", None),
        P(None, "tile", "layer"),
        P("tile", None),
        P("tile", "layer"),
        P("tile", "layer"),
        P("tile", "layer"),
    )
    out_specs = (P("layer", None, "tile", None), P())
    return jax.shard_map(shards, mesh=mesh, in_specs=in_specs, out_specs=out_specs, check_vma=False)
```

```python
import functools

import jax
import jax.numpy as jnp
from jax import lax
from jax.experimental import pallas as pl
from jax.experimental.pallas import tpu as pltpu
from jax.sharding import PartitionSpec as P

GROUPS = 512
LANES = 128
MESH = pl.DeviceIdType.MESH
F32 = jnp.float32


def kernel(
    tiles, scale,
    forc, vert, horiz, basal, label, mask,
    out, sens,
    v0, hh, bb, ll, mm, pack, vb, wl, fb, db, va, ip, gg, cp, mw, den, mid, cz, mr, mr2,
    et, eb, ht, hb, gs, gt, gb, zz, oh, part, s1, s2, s3, res,
    lsem, fsem, c_s, c_r, w_s, w_r, x_s, x_r, m1_s, m1_r, m2_s, m2_r,
    up_s, up_r, dn_s, dn_r, gu_s, gu_r, gd_s, gd_r, o_s, o_r, ol, r_s, r_r, g_s, g_r,
):
    nf = fb.shape[1]
    nh = fb.shape[0]
    half = nh // 2
    nrows, width = hh.shape
    blocks = width // LANES
    nz = min(8, tiles // 2)
    ny = tiles // (2 * nz)
    t = lax.axis_index("tile")
    l = lax.axis_index("layer")
    p = l // 2
    c = l - 2 * p
    z = t % nz
    x = 2 * ((t // nz) % 2) + p
    y = t // (2 * nz)
    partner = 2 * p + 1 - c
    cross = 2 * (1 - p) + c
    diag = 2 * (1 - p) + 1 - c

    def at_x(number):
        return t + nz * (number // 2 - (x // 2)), 2 * (number % 2)

    def remote(src, dst, ssem, rsem, tile, layer):
        return pltpu.make_async_remote_copy(
            src_ref=src, dst_ref=dst, send_sem=ssem, recv_sem=rsem,
            device_id=(tile, layer), device_id_type=MESH,
        )

    barrier = pltpu.get_barrier_semaphore()

    def greet(tile, layer):
        pl.semaphore_signal(barrier, inc=1, device_id=(tile, layer), device_id_type=MESH)

    greet(t, cross)
    greet(t, diag)
    greet(t, partner)
    other = t + nz * (1 - 2 * (x // 2))
    for layer in range(4):
        greet(other, layer)
    first = jnp.logical_and(z == 0, t > 0)
    last = jnp.logical_and(z == nz - 1, t < tiles - 1)

    @pl.when(first)
    def _():
        greet(t - 1, l)

    @pl.when(last)
    def _():
        greet(t + 1, l)

    for d in range(1, nz):
        greet(t + (z + d) % nz - z, l)
    for d in range(1, ny):
        greet(t + 2 * nz * ((y + d) % ny - y), l)

    local = [
        pltpu.make_async_copy(vert.at[0], v0, lsem.at[0]),
        pltpu.make_async_copy(horiz, hh, lsem.at[1]),
        pltpu.make_async_copy(basal, bb, lsem.at[2]),
        pltpu.make_async_copy(label, ll, lsem.at[3]),
        pltpu.make_async_copy(mask, mm, lsem.at[4]),
    ]
    for copy in local:
        copy.start()
    own = pltpu.make_async_copy(vert.at[pl.ds(7 * p, 9)], vb.at[l], lsem.at[5])
    own.start()
    stay = pltpu.make_async_copy(
        forc.at[:, pl.ds(c * nf, nf)], fb.at[pl.ds(c * half, half)], lsem.at[6]
    )
    stay.start()

    greeted = 7 + (nz - 1) + (ny - 1)
    pl.semaphore_wait(barrier, greeted + first.astype(jnp.int32) + last.astype(jnp.int32))

    def coefs(number, layer, far):
        rows9 = vert.at[pl.ds(7 * (1 - p), 9)] if far else vert.at[pl.ds(7 * p, 9)]
        return remote(rows9, vb.at[l], c_s.at[number], c_r.at[number], t, layer)

    spread = [coefs(0, cross, True), coefs(1, diag, True), coefs(2, partner, False)]
    for copy in spread:
        copy.start()
    swap = remote(
        forc.at[:, pl.ds((1 - c) * nf, nf)], fb.at[pl.ds(c * half, half)],
        fsem.at[0], fsem.at[1], t, partner,
    )
    swap.start()

    for copy in local:
        copy.wait()
    pack[0] = v0[...] * bb[...] * mm[...].astype(F32)
    pack[1] = ll[...].astype(F32)
    tags = [
        remote(pack, wl.at[l], w_s.at[k], w_r.at[k], t, layer)
        for k, layer in enumerate((cross, diag, partner))
    ]
    for copy in tags:
        copy.start()
    wl[l] = pack[...]

    @pl.when(t == 0)
    def _():
        ht[...] = jnp.zeros_like(ht)
        gt[...] = jnp.zeros_like(gt)

    @pl.when(t == tiles - 1)
    def _():
        hb[...] = jnp.zeros_like(hb)
        gb[...] = jnp.zeros_like(gb)

    own.wait()
    for copy in spread:
        copy.wait_recv()

    lower = (1 - p).astype(F32)

    def coupling(i):
        return jnp.concatenate([vb[q, i + p * (9 - 2 * i)] for q in range(blocks)], axis=1)

    h4 = 4.0 * hh[...]
    outer = jnp.concatenate([vb[q, 9 * p - p] for q in range(blocks)], axis=1) * lower
    prev = None
    unit = None
    for i in range(nh):
        inner = coupling(i + 1)
        pivot = outer + inner + h4
        if prev is not None:
            pivot = pivot - outer * prev
        inverse = 1.0 / pivot
        prev = inner * inverse
        scaled = outer * inverse
        unit = inverse * lower if unit is None else scaled * unit
        ip[i] = inverse
        gg[i] = scaled
        cp[i] = prev
        mw[i] = unit
        outer = inner
    mid[0] = prev
    mid[1] = unit
    middle = remote(mid, cz, x_s, x_r, t, cross)
    middle.start()

    def at(i):
        return i + p * (nh - 1 - 2 * i)

    stay.wait()
    swap.wait_recv()

    def mid1(f):
        return remote(fb.at[at(nh - 1), f], mr.at[f], m1_s.at[f], m1_r.at[f], t, cross)

    def mid2(f):
        return remote(db.at[nh - 1, f], mr2.at[f], m2_s.at[f], m2_r.at[f], t, cross)

    def up(f):
        return remote(et.at[f], hb.at[f], up_s.at[f], up_r.at[f], t - 1, l)

    def down(f):
        return remote(eb.at[f], ht.at[f], dn_s.at[f], dn_r.at[f], t + 1, l)

    ghost_up = remote(gs.at[0], gb, gu_s, gu_r, t - 1, l)
    ghost_down = remote(gs.at[1], gt, gd_s, gd_r, t + 1, l)

    def forward1(f, carry):
        d = None
        for i in range(nh):
            d_new = fb[at(i), f] * ip[i]
            d = d_new if d is None else d_new + gg[i] * d
            fb[at(i), f] = d
        mid1(f).start()
        return carry

    lax.fori_loop(0, nf, forward1, 0)

    for copy in tags:
        copy.wait_recv()

    def mark(r, row):
        low = row.astype(jnp.int32) % LANES
        groups = lax.broadcasted_iota(jnp.int32, (LANES, width), 0)
        oh[r] = (groups == low).astype(F32).astype(jnp.bfloat16)

    def label_row(r):
        return jnp.concatenate([wl[q, 1, r : r + 1, :] for q in range(blocks)], axis=1)

    for r in range(nrows // 2):
        mark(r, label_row(r))

    weight = jnp.concatenate([wl[q, 0] for q in range(blocks)], axis=1)
    factor = weight * hh[...]
    middle.wait_recv()
    inverse = 1.0 / (1.0 - mid[0] * cz[0])
    den[...] = inverse
    m = (mid[1] + mid[0] * cz[1]) * inverse
    for i in range(nh - 1, -1, -1):
        if i < nh - 1:
            m = mw[i] + cp[i] * m
        mi = m * factor
        mw[i] = mi
        gs[0, i : i + 1, :] = mi[0:1, :]
        gs[1, i : i + 1, :] = mi[nrows - 1 : nrows, :]
    gs[0, nh : nh + 1, :] = label_row(0)
    gs[1, nh : nh + 1, :] = label_row(nrows - 1)

    @pl.when(t > 0)
    def _():
        ghost_up.start()

    @pl.when(t < tiles - 1)
    def _():
        ghost_down.start()

    for r in range(nrows // 2, nrows):
        mark(r, label_row(r))

    shape = (nrows, width)
    rows = lax.broadcasted_iota(jnp.int32, shape, 0)
    columns = lax.broadcasted_iota(jnp.int32, shape, 1)

    def backward1(f, carry):
        mid1(f).wait()
        v = None
        total = None
        for i in range(nh - 1, -1, -1):
            if v is None:
                v = (fb[at(i), f] + cp[i] * mr[f]) * den[...]
            else:
                v = fb[at(i), f] + cp[i] * v
            fb[at(i), f] = v
            et[f, i : i + 1, :] = v[0:1, :]
            eb[f, i : i + 1, :] = v[nrows - 1 : nrows, :]
            above = jnp.where(rows == 0, 0.0, pltpu.roll(v, 1, axis=0))
            below = jnp.where(rows == nrows - 1, 0.0, pltpu.roll(v, nrows - 1, axis=0))
            left = jnp.where(columns == 0, 0.0, pltpu.roll(v, 1, axis=1))
            right = jnp.where(columns == width - 1, 0.0, pltpu.roll(v, width - 1, axis=1))
            near = (above + below) + (left + right)
            db[i, f] = near
            total = mw[i] * near if total is None else total + mw[i] * near

        @pl.when(t > 0)
        def _():
            up(f).start()

        @pl.when(t < tiles - 1)
        def _():
            down(f).start()

        va[f] = total + (weight * lower) * v
        return carry

    lax.fori_loop(0, nf, backward1, 0)

    for f in range(nf):
        v = va[f]
        for r in range(nrows):
            zz[r, f : f + 1, :] = v[r : r + 1, :]

    @pl.when(t > 0)
    def _():
        ghost_down.wait_recv()

    @pl.when(t < tiles - 1)
    def _():
        ghost_up.wait_recv()

    mark(nrows, gt[nh : nh + 1, :])
    mark(nrows + 1, gb[nh : nh + 1, :])
    for f in range(nf):
        zz[nrows, f : f + 1, :] = jnp.sum(gt[0:nh, :] * et[f], axis=0, keepdims=True)
        zz[nrows + 1, f : f + 1, :] = jnp.sum(gb[0:nh, :] * eb[f], axis=0, keepdims=True)
    total = jnp.zeros((12 * nf, LANES), F32)
    for r in range(nrows + 2):
        if r < nrows:
            row = label_row(r)
        else:
            row = (gt if r == nrows else gb)[nh : nh + 1, :]
        high = row.astype(jnp.int32) // LANES
        v = zz[r]
        apart = jnp.concatenate([jnp.where(high == g, v, 0.0) for g in range(4)], axis=0)
        a0 = apart.astype(jnp.bfloat16)
        rest = apart - a0.astype(F32)
        a1 = rest.astype(jnp.bfloat16)
        a2 = (rest - a1.astype(F32)).astype(jnp.bfloat16)
        total += lax.dot_general(
            jnp.concatenate([a0, a1, a2], axis=0), oh[r],
            (((1,), (1,)), ((), ())), preferred_element_type=F32,
        )
    n = 4 * nf
    sums = (total[2 * n :] + total[n : 2 * n]) + total[:n]
    for g in range(4):
        part[g] = sums[g * nf : (g + 1) * nf]

    s1[x] = part[x]
    stage1 = []
    for d in range(1, 4):
        there = (x + d) % 4
        tile, layer = at_x(there)
        stage1.append(
            remote(part.at[there], s1.at[x], r_s.at[0, d - 1], r_r.at[0, d - 1], tile, layer + c)
        )
    for copy in stage1:
        copy.start()

    def exchange(number, buffer, size, mine, stride):
        return [
            remote(buffer.at[mine], buffer.at[mine], r_s.at[number, d - 1], r_r.at[number, d - 1],
                   t + stride * ((mine + d) % size - mine), l)
            for d in range(1, size)
        ]

    stage2 = exchange(1, s2, nz, z, 1)
    stage3 = exchange(2, s3, ny, y, 2 * nz)

    def gathers():
        copies = []
        for d in range(4):
            tile, layer = at_x((x + d) % 4)
            for dc in range(2):
                if d or dc:
                    copies.append(
                        remote(res.at[c, x], res.at[c, x], g_s.at[d, dc], g_r.at[d, dc],
                               tile, layer + (c + dc) % 2)
                    )
        return copies

    def forward2(f, carry):
        @pl.when(t > 0)
        def _():
            down(f).wait_recv()

        @pl.when(t < tiles - 1)
        def _():
            up(f).wait_recv()

        d = None
        for i in range(nh):
            near = db[i, f] + jnp.where(rows == 0, ht[f, i : i + 1, :], 0.0)
            near = near + jnp.where(rows == nrows - 1, hb[f, i : i + 1, :], 0.0)
            d_new = (hh[...] * near) * ip[i]
            d = d_new if d is None else d_new + gg[i] * d
            db[i, f] = d
        mid2(f).start()
        return carry

    def give(f):
        return remote(
            fb.at[pl.ds((1 - c) * half, half), f], out.at[:, c * nf + f],
            o_s.at[f], o_r.at[f], t, partner,
        )

    def keep(f):
        return pltpu.make_async_copy(
            fb.at[pl.ds(c * half, half), f], out.at[:, c * nf + f], ol.at[f]
        )

    def backward2(f, carry):
        mid2(f).wait()
        v = None
        for i in range(nh - 1, -1, -1):
            if v is None:
                v = (db[i, f] + cp[i] * mr2[f]) * den[...]
            else:
                v = db[i, f] + cp[i] * v
            fb[at(i), f] = fb[at(i), f] + v
        give(f).start()
        keep(f).start()
        return carry

    for copy in stage1:
        copy.wait()
    s2[z] = (s1[0] + s1[1]) + (s1[2] + s1[3])
    for copy in stage2:
        copy.start()

    lax.fori_loop(0, nf, forward2, 0)

    def folded(buffer, size):
        value = buffer[0]
        for k in range(1, size):
            value = value + buffer[k]
        return value

    for copy in stage2:
        copy.wait()
    s3[y] = folded(s2, nz)
    for copy in stage3:
        copy.start()
    for copy in stage3:
        copy.wait()
    res[c, x] = folded(s3, ny) * scale
    for copy in gathers():
        copy.start()

    lax.fori_loop(0, nf, backward2, 0)

    for d in range(4):
        for dc in range(2):
            if d or dc:
                source = res.at[(c + dc) % 2, (x - d + 4) % 4]
                remote(source, source, g_s.at[d, dc], g_r.at[d, dc], t, partner).wait_recv()
    for core in range(2):
        for g in range(4):
            sens[core * nf : (core + 1) * nf, g * LANES : (g + 1) * LANES] = res[core, g]

    for copy in spread + tags + [swap, middle] + gathers():
        copy.wait_send()

    @pl.when(t > 0)
    def _():
        ghost_up.wait_send()

    @pl.when(t < tiles - 1)
    def _():
        ghost_down.wait_send()

    def drain(f, carry):
        @pl.when(t > 0)
        def _():
            up(f).wait_send()

        @pl.when(t < tiles - 1)
        def _():
            down(f).wait_send()

        keep(f).wait()
        give(f).wait()
        return carry

    lax.fori_loop(0, nf, drain, 0)


def shards(forcing, vert_coupling, horiz_coupling, basal_velocity, group_label, ice_mask):
    tiles = lax.axis_size("tile")
    layers, functionals, rows, width = forcing.shape
    nf = functionals // 2
    nh = 2 * layers
    nz = min(8, tiles // 2)
    ny = tiles // (2 * nz)
    scale = -((tiles * rows * width / GROUPS) ** (-0.5))
    dma = pltpu.SemaphoreType.DMA
    vmem = pltpu.VMEM
    field = vmem((nh, nf, rows, width), F32)
    per_f = vmem((nf, rows, width), F32)
    per_layer = vmem((nh, rows, width), F32)
    flat = vmem((rows, width), F32)
    pair = vmem((2, rows, width), F32)
    tile = vmem((rows, LANES), F32)
    whole = vmem((rows, LANES), jnp.int32)
    edge = vmem((nf, nh, width), F32)
    ghost = vmem((nh + 1, width), F32)
    pieces = vmem((4, nf, LANES), F32)
    scratch = [
        tile, flat, tile, whole, whole,
        vmem((2, rows, LANES), F32), vmem((4, 9, rows, LANES), F32), vmem((4, 2, rows, LANES), F32),
        field, field, per_f, per_layer, per_layer, per_layer, per_layer,
        flat, pair, pair, per_f, per_f,
        edge, edge, edge, edge, vmem((2, nh + 1, width), F32), ghost, ghost,
        vmem((rows + 2, nf, width), F32), vmem((rows + 2, LANES, width), jnp.bfloat16),
        pieces, pieces, vmem((nz, nf, LANES), F32), vmem((ny, nf, LANES), F32),
        vmem((2, 4, nf, LANES), F32),
        dma((7,)), dma((2,)), dma((3,)), dma((3,)), dma((3,)), dma((3,)), dma, dma,
        dma((nf,)), dma((nf,)), dma((nf,)), dma((nf,)),
        dma((nf,)), dma((nf,)), dma((nf,)), dma((nf,)),
        dma, dma, dma, dma,
        dma((nf,)), dma((nf,)), dma((nf,)),
        dma((3, 8)), dma((3, 8)), dma((4, 2)), dma((4, 2)),
    ]
    operands = (forcing, vert_coupling, horiz_coupling, basal_velocity, group_label, ice_mask)
    return pl.pallas_call(
        functools.partial(kernel, tiles, scale),
        out_shape=(
            jax.ShapeDtypeStruct(forcing.shape, F32),
            jax.ShapeDtypeStruct((functionals, GROUPS), F32),
        ),
        in_specs=[pl.BlockSpec(memory_space=pltpu.HBM)] * 6,
        out_specs=(pl.BlockSpec(memory_space=pl.ANY), pl.BlockSpec(memory_space=pltpu.VMEM)),
        scratch_shapes=scratch,
        compiler_params=pltpu.CompilerParams(
            collective_id=0, has_side_effects=True, vmem_limit_bytes=32 * 1024 * 1024
        ),
        name="sweeps",
    )(*[pltpu.with_memory_space_constraint(operand, pltpu.HBM) for operand in operands])


def solution(mesh):
    in_specs = (
        P("layer", None, "tile", None),
        P(None, "tile", "layer"),
        P("tile", None),
        P("tile", "layer"),
        P("tile", "layer"),
        P("tile", "layer"),
    )
    out_specs = (P("layer", None, "tile", None), P())
    return jax.shard_map(shards, mesh=mesh, in_specs=in_specs, out_specs=out_specs, check_vma=False)
```

```python
import functools

import jax
import jax.numpy as jnp
from jax import lax
from jax.experimental import pallas as pl
from jax.experimental.pallas import tpu as pltpu
from jax.sharding import PartitionSpec as P

GROUPS = 512
LANES = 128
MESH = pl.DeviceIdType.MESH
F32 = jnp.float32


def kernel(
    tiles, scale,
    forc, vert, horiz, basal, label, mask,
    out, sens,
    v0, hh, bb, ll, mm, lf, pe, pack, vb, wl, fb, gf, db, va, ip, gg, cp, mw, den,
    mid, cz, mr, mr2, gs, gc, gip, ggg, gcp, gmid, gcz, gmr, zz, oh, part, s1, s2, s3, res,
    lsem, fsem, c_s, c_r, w_s, w_r, x_s, x_r, m1_s, m1_r, m2_s, m2_r,
    e_s, e_r, q_s, q_r, gx_s, gx_r, gm_s, gm_r, o_s, o_r, ol, r_s, r_r, g_s, g_r,
):
    nf = fb.shape[1]
    nh = fb.shape[0]
    half = nh // 2
    nrows, width = hh.shape
    blocks = width // LANES
    nz = min(8, tiles // 2)
    ny = tiles // (2 * nz)
    t = lax.axis_index("tile")
    l = lax.axis_index("layer")
    p = l // 2
    c = l - 2 * p
    z = t % nz
    x = 2 * ((t // nz) % 2) + p
    y = t // (2 * nz)
    partner = 2 * p + 1 - c
    cross = 2 * (1 - p) + c
    diag = 2 * (1 - p) + 1 - c

    def at_x(number):
        return t + nz * (number // 2 - (x // 2)), 2 * (number % 2)

    def remote(src, dst, ssem, rsem, tile, layer):
        return pltpu.make_async_remote_copy(
            src_ref=src, dst_ref=dst, send_sem=ssem, recv_sem=rsem,
            device_id=(tile, layer), device_id_type=MESH,
        )

    barrier = pltpu.get_barrier_semaphore()

    def greet(tile, layer):
        pl.semaphore_signal(barrier, inc=1, device_id=(tile, layer), device_id_type=MESH)

    greet(t, cross)
    greet(t, diag)
    greet(t, partner)
    other = t + nz * (1 - 2 * (x // 2))
    for layer in range(4):
        greet(other, layer)
    first = jnp.logical_and(z == 0, t > 0)
    last = jnp.logical_and(z == nz - 1, t < tiles - 1)

    above = t > 0
    under = t < tiles - 1

    @pl.when(above)
    def _():
        greet(t - 1, partner)

    @pl.when(under)
    def _():
        greet(t + 1, partner)

    @pl.when(first)
    def _():
        greet(t - 1, l)

    @pl.when(last)
    def _():
        greet(t + 1, l)

    for d in range(1, nz):
        greet(t + (z + d) % nz - z, l)
    for d in range(1, ny):
        greet(t + 2 * nz * ((y + d) % ny - y), l)

    whole = pltpu.make_async_copy(forc, lf, lsem.at[7])
    whole.start()
    local = [
        pltpu.make_async_copy(vert.at[0], v0, lsem.at[0]),
        pltpu.make_async_copy(horiz, hh, lsem.at[1]),
        pltpu.make_async_copy(basal, bb, lsem.at[2]),
        pltpu.make_async_copy(label, ll, lsem.at[3]),
        pltpu.make_async_copy(mask, mm, lsem.at[4]),
    ]
    for copy in local:
        copy.start()
    own = pltpu.make_async_copy(vert.at[pl.ds(7 * p, 9)], vb.at[l], lsem.at[5])
    own.start()
    stay = pltpu.make_async_copy(
        forc.at[:, pl.ds(c * nf, nf)], fb.at[pl.ds(c * half, half)], lsem.at[6]
    )
    stay.start()

    whole.wait()

    def pick(j, carry):
        for core in range(2):
            for f in range(nf):
                block = lf[j, core * nf + f]
                pe[0, core, j, f : f + 1, :] = block[0:1, :]
                pe[1, core, j, f : f + 1, :] = block[nrows - 1 : nrows, :]
        return carry

    lax.fori_loop(0, half, pick, 0)

    greeted = 7 + (nz - 1) + (ny - 1)
    for extra in (above, under, first, last):
        greeted = greeted + extra.astype(jnp.int32)
    pl.semaphore_wait(barrier, greeted)

    def coefs(number, layer, far):
        rows9 = vert.at[pl.ds(7 * (1 - p), 9)] if far else vert.at[pl.ds(7 * p, 9)]
        return remote(rows9, vb.at[l], c_s.at[number], c_r.at[number], t, layer)

    spread = [coefs(0, cross, True), coefs(1, diag, True), coefs(2, partner, False)]
    for copy in spread:
        copy.start()
    swap = remote(
        forc.at[:, pl.ds((1 - c) * nf, nf)], fb.at[pl.ds(c * half, half)],
        fsem.at[0], fsem.at[1], t, partner,
    )
    swap.start()

    def edge(side, core):
        return remote(
            pe.at[side, core], gf.at[1 - side, pl.ds(c * half, half)],
            e_s.at[side, core], e_r.at[1 - side, c], t + 2 * side - 1, 2 * p + core,
        )

    def edge_arrival(side, core):
        return remote(
            pe.at[1 - side, core], gf.at[side, pl.ds(core * half, half)],
            e_s.at[1 - side, core], e_r.at[side, core], t, partner,
        )

    sides = ((0, above), (1, under))

    for side, there in sides:
        @pl.when(there)
        def _():
            for core in range(2):
                edge(side, core).start()

    for copy in local:
        copy.wait()
    pack[0] = v0[...] * bb[...] * mm[...].astype(F32)
    pack[1] = ll[...].astype(F32)
    tags = [
        remote(pack, wl.at[l], w_s.at[k], w_r.at[k], t, layer)
        for k, layer in enumerate((cross, diag, partner))
    ]
    for copy in tags:
        copy.start()
    wl[l] = pack[...]

    for side, there in sides:
        @pl.when(jnp.logical_not(there))
        def _():
            gf[side] = jnp.zeros(gf.shape[1:], F32)
            gc[side] = jnp.zeros(gc.shape[1:], F32)
            gc[side, nh + 1 : nh + 2, :] = jnp.ones((1, width), F32)

    own.wait()
    for copy in spread:
        copy.wait_recv()

    lower = (1 - p).astype(F32)

    def coupling(i):
        return jnp.concatenate([vb[q, i + p * (9 - 2 * i)] for q in range(blocks)], axis=1)

    h4 = 4.0 * hh[...]
    outer = jnp.concatenate([vb[q, 9 * p - p] for q in range(blocks)], axis=1) * lower
    prev = None
    unit = None
    for side in range(2):
        row = side * (nrows - 1)
        gs[side, 0:1, :] = outer[row : row + 1, :]
        gs[side, nh + 1 : nh + 2, :] = hh[row : row + 1, :]
    for i in range(nh):
        inner = coupling(i + 1)
        pivot = outer + inner + h4
        if prev is not None:
            pivot = pivot - outer * prev
        inverse = 1.0 / pivot
        prev = inner * inverse
        scaled = outer * inverse
        unit = inverse * lower if unit is None else scaled * unit
        ip[i] = inverse
        gg[i] = scaled
        cp[i] = prev
        mw[i] = unit
        outer = inner
        for side in range(2):
            row = side * (nrows - 1)
            gs[side, i + 1 : i + 2, :] = inner[row : row + 1, :]
    mid[0] = prev
    mid[1] = unit
    middle = remote(mid, cz, x_s, x_r, t, cross)
    middle.start()

    def tell(side):
        return remote(
            gs.at[side], gc.at[1 - side], q_s.at[side], q_r.at[1 - side], t + 2 * side - 1, l
        )

    def told(side):
        return remote(gs.at[1 - side], gc.at[side], q_s.at[1 - side], q_r.at[side], t, partner)

    for side, there in sides:
        @pl.when(there)
        def _():
            tell(side).start()

    def at(i):
        return i + p * (nh - 1 - 2 * i)

    stay.wait()
    swap.wait_recv()

    def mid1(f):
        return remote(fb.at[at(nh - 1), f], mr.at[f], m1_s.at[f], m1_r.at[f], t, cross)

    def mid2(f):
        return remote(db.at[nh - 1, f], mr2.at[f], m2_s.at[f], m2_r.at[f], t, cross)

    def forward1(f, carry):
        d = None
        for i in range(nh):
            d_new = fb[at(i), f] * ip[i]
            d = d_new if d is None else d_new + gg[i] * d
            fb[at(i), f] = d
        mid1(f).start()
        return carry

    lax.fori_loop(0, nf, forward1, 0)

    for copy in tags:
        copy.wait_recv()

    def mark(r, row):
        low = row.astype(jnp.int32) % LANES
        groups = lax.broadcasted_iota(jnp.int32, (LANES, width), 0)
        oh[r] = (groups == low).astype(F32).astype(jnp.bfloat16)

    def label_row(r):
        return jnp.concatenate([wl[q, 1, r : r + 1, :] for q in range(blocks)], axis=1)

    for r in range(nrows // 2):
        mark(r, label_row(r))

    weight = jnp.concatenate([wl[q, 0] for q in range(blocks)], axis=1)
    middle.wait_recv()
    inverse = 1.0 / (1.0 - mid[0] * cz[0])
    den[...] = inverse
    m = (mid[1] + mid[0] * cz[1]) * inverse
    for i in range(nh - 1, -1, -1):
        if i < nh - 1:
            m = mw[i] + cp[i] * m
        mw[i] = m * weight

    for side, there in sides:
        @pl.when(there)
        def _():
            told(side).wait_recv()
            for core in range(2):
                edge_arrival(side, core).wait_recv()

    def gmid1(side):
        return remote(
            gf.at[side, at(nh - 1)], gmr.at[side], gm_s.at[side], gm_r.at[side], t, cross
        )

    for side in range(2):
        h4 = 4.0 * gc[side, nh + 1 : nh + 2, :]
        prev = None
        for i in range(nh):
            outer = gc[side, i : i + 1, :]
            inner = gc[side, i + 1 : i + 2, :]
            pivot = outer + inner + h4
            if prev is not None:
                pivot = pivot - outer * prev
            inverse = 1.0 / pivot
            prev = inner * inverse
            gip[side, i : i + 1, :] = inverse
            ggg[side, i : i + 1, :] = outer * inverse
            gcp[side, i : i + 1, :] = prev
        gmid[side] = prev
    gmiddle = remote(gmid, gcz, gx_s, gx_r, t, cross)
    gmiddle.start()
    for side in range(2):
        d = None
        for i in range(nh):
            d_new = gf[side, at(i)] * gip[side, i : i + 1, :]
            d = d_new if d is None else d_new + ggg[side, i : i + 1, :] * d
            gf[side, at(i)] = d
        gmid1(side).start()

    for r in range(nrows // 2, nrows):
        mark(r, label_row(r))

    def backward1(f, carry):
        mid1(f).wait()
        v = None
        for i in range(nh - 1, -1, -1):
            if v is None:
                v = (fb[at(i), f] + cp[i] * mr[f]) * den[...]
            else:
                v = fb[at(i), f] + cp[i] * v
            fb[at(i), f] = v
        return carry

    lax.fori_loop(0, nf, backward1, 0)

    gmiddle.wait_recv()
    for side in range(2):
        gmid1(side).wait()
        v = None
        for i in range(nh - 1, -1, -1):
            factor = gcp[side, i : i + 1, :]
            if v is None:
                v = (gf[side, at(i)] + factor * gmr[side]) * (1.0 / (1.0 - factor * gcz[side]))
            else:
                v = gf[side, at(i)] + factor * v
            gf[side, at(i)] = v

    shape = (nrows, width)
    rows = lax.broadcasted_iota(jnp.int32, shape, 0)
    columns = lax.broadcasted_iota(jnp.int32, shape, 1)

    def forward2(f, carry):
        d = None
        total = None
        for i in range(nh):
            v = fb[at(i), f]
            before = jnp.where(
                rows == 0, gf[0, at(i), pl.ds(f, 1), :], pltpu.roll(v, 1, axis=0)
            )
            after = jnp.where(
                rows == nrows - 1, gf[1, at(i), pl.ds(f, 1), :], pltpu.roll(v, nrows - 1, axis=0)
            )
            left = jnp.where(columns == 0, 0.0, pltpu.roll(v, 1, axis=1))
            right = jnp.where(columns == width - 1, 0.0, pltpu.roll(v, width - 1, axis=1))
            residual = hh[...] * ((before + after) + (left + right))
            term = mw[i] * residual
            if i == 0:
                total = term + (weight * lower) * v
            else:
                total = total + term
            d_new = residual * ip[i]
            d = d_new if d is None else d_new + gg[i] * d
            db[i, f] = d
        va[f] = total
        mid2(f).start()
        return carry

    lax.fori_loop(0, nf, forward2, 0)

    for f in range(nf):
        v = va[f]
        for r in range(nrows):
            zz[r, f : f + 1, :] = v[r : r + 1, :]

    total = jnp.zeros((12 * nf, LANES), F32)
    for r in range(nrows):
        high = label_row(r).astype(jnp.int32) // LANES
        v = zz[r]
        apart = jnp.concatenate([jnp.where(high == g, v, 0.0) for g in range(4)], axis=0)
        a0 = apart.astype(jnp.bfloat16)
        rest = apart - a0.astype(F32)
        a1 = rest.astype(jnp.bfloat16)
        a2 = (rest - a1.astype(F32)).astype(jnp.bfloat16)
        total += lax.dot_general(
            jnp.concatenate([a0, a1, a2], axis=0), oh[r],
            (((1,), (1,)), ((), ())), preferred_element_type=F32,
        )
    n = 4 * nf
    sums = (total[2 * n :] + total[n : 2 * n]) + total[:n]
    for g in range(4):
        part[g] = sums[g * nf : (g + 1) * nf]

    s1[x] = part[x]
    stage1 = []
    for d in range(1, 4):
        there = (x + d) % 4
        tile, layer = at_x(there)
        stage1.append(
            remote(part.at[there], s1.at[x], r_s.at[0, d - 1], r_r.at[0, d - 1], tile, layer + c)
        )
    for copy in stage1:
        copy.start()

    def exchange(number, buffer, size, mine, stride):
        return [
            remote(buffer.at[mine], buffer.at[mine], r_s.at[number, d - 1], r_r.at[number, d - 1],
                   t + stride * ((mine + d) % size - mine), l)
            for d in range(1, size)
        ]

    stage2 = exchange(1, s2, nz, z, 1)
    stage3 = exchange(2, s3, ny, y, 2 * nz)

    def gathers():
        copies = []
        for d in range(4):
            tile, layer = at_x((x + d) % 4)
            for dc in range(2):
                if d or dc:
                    copies.append(
                        remote(res.at[c, x], res.at[c, x], g_s.at[d, dc], g_r.at[d, dc],
                               tile, layer + (c + dc) % 2)
                    )
        return copies

    def give(f):
        return remote(
            fb.at[pl.ds((1 - c) * half, half), f], out.at[:, c * nf + f],
            o_s.at[f], o_r.at[f], t, partner,
        )

    def keep(f):
        return pltpu.make_async_copy(
            fb.at[pl.ds(c * half, half), f], out.at[:, c * nf + f], ol.at[f]
        )

    def backward2(f, carry):
        mid2(f).wait()
        v = None
        for i in range(nh - 1, -1, -1):
            if v is None:
                v = (db[i, f] + cp[i] * mr2[f]) * den[...]
            else:
                v = db[i, f] + cp[i] * v
            fb[at(i), f] = fb[at(i), f] + v
        give(f).start()
        keep(f).start()
        return carry

    for copy in stage1:
        copy.wait()
    s2[z] = (s1[0] + s1[1]) + (s1[2] + s1[3])
    for copy in stage2:
        copy.start()

    lax.fori_loop(0, nf, backward2, 0)

    def folded(buffer, size):
        value = buffer[0]
        for k in range(1, size):
            value = value + buffer[k]
        return value

    for copy in stage2:
        copy.wait()
    s3[y] = folded(s2, nz)
    for copy in stage3:
        copy.start()
    for copy in stage3:
        copy.wait()
    res[c, x] = folded(s3, ny) * scale
    for copy in gathers():
        copy.start()

    for d in range(4):
        for dc in range(2):
            if d or dc:
                source = res.at[(c + dc) % 2, (x - d + 4) % 4]
                remote(source, source, g_s.at[d, dc], g_r.at[d, dc], t, partner).wait_recv()
    for core in range(2):
        for g in range(4):
            sens[core * nf : (core + 1) * nf, g * LANES : (g + 1) * LANES] = res[core, g]

    for copy in spread + tags + [swap, middle, gmiddle] + gathers():
        copy.wait_send()
    for side, there in sides:
        @pl.when(there)
        def _():
            tell(side).wait_send()
            for core in range(2):
                edge(side, core).wait_send()

    def drain(f, carry):
        keep(f).wait()
        give(f).wait()
        return carry

    lax.fori_loop(0, nf, drain, 0)


def shards(forcing, vert_coupling, horiz_coupling, basal_velocity, group_label, ice_mask):
    tiles = lax.axis_size("tile")
    layers, functionals, rows, width = forcing.shape
    nf = functionals // 2
    nh = 2 * layers
    nz = min(8, tiles // 2)
    ny = tiles // (2 * nz)
    scale = -((tiles * rows * width / GROUPS) ** (-0.5))
    dma = pltpu.SemaphoreType.DMA
    vmem = pltpu.VMEM
    field = vmem((nh, nf, rows, width), F32)
    per_f = vmem((nf, rows, width), F32)
    per_layer = vmem((nh, rows, width), F32)
    flat = vmem((rows, width), F32)
    pair = vmem((2, rows, width), F32)
    tile = vmem((rows, LANES), F32)
    whole = vmem((rows, LANES), jnp.int32)
    ghost = vmem((2, nh + 2, width), F32)
    ghost_coef = vmem((2, nh, width), F32)
    ghost_row = vmem((2, 1, width), F32)
    pieces = vmem((4, nf, LANES), F32)
    scratch = [
        tile, flat, tile, whole, whole,
        vmem(forcing.shape, F32), vmem((2, 2, layers, nf, width), F32),
        vmem((2, rows, LANES), F32), vmem((4, 9, rows, LANES), F32), vmem((4, 2, rows, LANES), F32),
        field, vmem((2, nh, nf, width), F32), field, per_f,
        per_layer, per_layer, per_layer, per_layer, flat,
        pair, pair, per_f, per_f,
        ghost, ghost, ghost_coef, ghost_coef, ghost_coef, ghost_row, ghost_row,
        vmem((2, nf, width), F32),
        vmem((rows, nf, width), F32), vmem((rows, LANES, width), jnp.bfloat16),
        pieces, pieces, vmem((nz, nf, LANES), F32), vmem((ny, nf, LANES), F32),
        vmem((2, 4, nf, LANES), F32),
        dma((8,)), dma((2,)), dma((3,)), dma((3,)), dma((3,)), dma((3,)), dma, dma,
        dma((nf,)), dma((nf,)), dma((nf,)), dma((nf,)),
        dma((2, 2)), dma((2, 2)), dma((2,)), dma((2,)), dma, dma, dma((2,)), dma((2,)),
        dma((nf,)), dma((nf,)), dma((nf,)),
        dma((3, 8)), dma((3, 8)), dma((4, 2)), dma((4, 2)),
    ]
    operands = (forcing, vert_coupling, horiz_coupling, basal_velocity, group_label, ice_mask)
    return pl.pallas_call(
        functools.partial(kernel, tiles, scale),
        out_shape=(
            jax.ShapeDtypeStruct(forcing.shape, F32),
            jax.ShapeDtypeStruct((functionals, GROUPS), F32),
        ),
        in_specs=[pl.BlockSpec(memory_space=pltpu.HBM)] * 6,
        out_specs=(pl.BlockSpec(memory_space=pl.ANY), pl.BlockSpec(memory_space=pltpu.VMEM)),
        scratch_shapes=scratch,
        compiler_params=pltpu.CompilerParams(
            collective_id=0, has_side_effects=True, vmem_limit_bytes=32 * 1024 * 1024
        ),
        name="sweeps",
    )(*[pltpu.with_memory_space_constraint(operand, pltpu.HBM) for operand in operands])


def solution(mesh):
    in_specs = (
        P("layer", None, "tile", None),
        P(None, "tile", "layer"),
        P("tile", None),
        P("tile", "layer"),
        P("tile", "layer"),
        P("tile", "layer"),
    )
    out_specs = (P("layer", None, "tile", None), P())
    return jax.shard_map(shards, mesh=mesh, in_specs=in_specs, out_specs=out_specs, check_vma=False)
```

```python
import functools

import jax
import jax.numpy as jnp
from jax import lax
from jax.experimental import pallas as pl
from jax.experimental.pallas import tpu as pltpu
from jax.sharding import PartitionSpec as P

GROUPS = 512
LANES = 128
MESH = pl.DeviceIdType.MESH
F32 = jnp.float32


def kernel(
    tiles, scale,
    forc, vert, horiz, basal, label, mask,
    out, sens,
    v0, hh, bb, ll, mm, pack, vb, wl, fb, db, va, ip, gg, cp, mw, den, mr, mr2,
    et, eb, ht, hb, gs, gt, gb, zz, oh, part, s1, s2, s3, res,
    lsem, fsem, c_s, c_r, w_s, w_r, m1_s, m1_r, m2_s, m2_r,
    up_s, up_r, dn_s, dn_r, gu_s, gu_r, gd_s, gd_r, o_s, o_r, ol, r_s, r_r, g_s, g_r,
):
    nf = fb.shape[1]
    nh = fb.shape[0]
    half = nh // 2
    nrows, width = hh.shape
    blocks = width // LANES
    nz = min(8, tiles // 2)
    ny = tiles // (2 * nz)
    t = lax.axis_index("tile")
    l = lax.axis_index("layer")
    p = l // 2
    c = l - 2 * p
    z = t % nz
    x = 2 * ((t // nz) % 2) + p
    y = t // (2 * nz)
    partner = 2 * p + 1 - c
    cross = 2 * (1 - p) + c
    diag = 2 * (1 - p) + 1 - c

    def at_x(number):
        return t + nz * (number // 2 - (x // 2)), 2 * (number % 2)

    def remote(src, dst, ssem, rsem, tile, layer):
        return pltpu.make_async_remote_copy(
            src_ref=src, dst_ref=dst, send_sem=ssem, recv_sem=rsem,
            device_id=(tile, layer), device_id_type=MESH,
        )

    barrier = pltpu.get_barrier_semaphore()

    def greet(tile, layer):
        pl.semaphore_signal(barrier, inc=1, device_id=(tile, layer), device_id_type=MESH)

    greet(t, cross)
    greet(t, diag)
    greet(t, partner)
    other = t + nz * (1 - 2 * (x // 2))
    for layer in range(4):
        greet(other, layer)
    first = jnp.logical_and(z == 0, t > 0)
    last = jnp.logical_and(z == nz - 1, t < tiles - 1)
    inner_tile = jnp.logical_not(jnp.logical_or(first, last))

    @pl.when(first)
    def _():
        greet(t - 1, l)

    @pl.when(last)
    def _():
        greet(t + 1, l)

    for d in range(1, nz):
        greet(t + (z + d) % nz - z, l)
    for d in range(1, ny):
        greet(t + 2 * nz * ((y + d) % ny - y), l)

    local = [
        pltpu.make_async_copy(vert.at[0], v0, lsem.at[0]),
        pltpu.make_async_copy(horiz, hh, lsem.at[1]),
        pltpu.make_async_copy(basal, bb, lsem.at[2]),
        pltpu.make_async_copy(label, ll, lsem.at[3]),
        pltpu.make_async_copy(mask, mm, lsem.at[4]),
    ]
    for copy in local:
        copy.start()
    own = pltpu.make_async_copy(vert, vb.at[l], lsem.at[5])
    own.start()
    stay = pltpu.make_async_copy(
        forc.at[:, pl.ds(c * nf, nf)], fb.at[pl.ds(c * half, half)], lsem.at[6]
    )
    stay.start()

    greeted = 7 + (nz - 1) + (ny - 1)
    pl.semaphore_wait(barrier, greeted + first.astype(jnp.int32) + last.astype(jnp.int32))

    def coefs(number, layer, chip, late):
        some = pl.ds(9 * (1 - chip), 7) if late else pl.ds(7 * chip, 9)
        return remote(
            vert.at[some], vb.at[l, some], c_s.at[number], c_r.at[number], t, layer
        )

    def coefs_arrival(number, late):
        some = pl.ds(9 * (1 - p), 7) if late else pl.ds(7 * p, 9)
        return remote(vert.at[some], vb.at[l, some], c_s.at[number], c_r.at[number], t, partner)

    spread = [
        coefs(0, cross, 1 - p, False), coefs(1, diag, 1 - p, False), coefs(2, partner, p, False)
    ]
    spread_late = [
        coefs(3, cross, 1 - p, True), coefs(4, diag, 1 - p, True), coefs(5, partner, p, True)
    ]
    for copy in spread:
        copy.start()
    swap = remote(
        forc.at[:, pl.ds((1 - c) * nf, nf)], fb.at[pl.ds(c * half, half)],
        fsem.at[0], fsem.at[1], t, partner,
    )
    swap.start()
    for copy in spread_late:
        copy.start()

    for copy in local:
        copy.wait()
    pack[0] = v0[...] * bb[...] * mm[...].astype(F32)
    pack[1] = ll[...].astype(F32)
    tags = [
        remote(pack, wl.at[l], w_s.at[k], w_r.at[k], t, layer)
        for k, layer in enumerate((cross, diag, partner))
    ]
    for copy in tags:
        copy.start()
    wl[l] = pack[...]

    @pl.when(t == 0)
    def _():
        ht[...] = jnp.zeros_like(ht)
        gt[...] = jnp.zeros_like(gt)

    @pl.when(t == tiles - 1)
    def _():
        hb[...] = jnp.zeros_like(hb)
        gb[...] = jnp.zeros_like(gb)

    own.wait()
    for number in range(3):
        coefs_arrival(number, False).wait_recv()

    h4 = 4.0 * hh[...]

    def coupling(i, chip):
        value = jnp.concatenate(
            [vb[q, (i if i else 15 * chip) + chip * (16 - 2 * i if i else 0)] for q in range(blocks)],
            axis=1,
        )
        return value if i else value * (1 - chip).astype(F32)

    def pivots(chip):
        outer = coupling(0, chip)
        prev = None
        for i in range(nh):
            inner = coupling(i + 1, chip)
            pivot = outer + inner + h4
            if prev is not None:
                pivot = pivot - outer * prev
            inverse = 1.0 / pivot
            prev = inner * inverse
            yield inverse, outer * inverse, prev
            outer = inner

    lower = (1 - p).astype(F32)
    for i, (inverse, scaled, ahead) in enumerate(pivots(p)):
        ip[i] = inverse
        gg[i] = scaled
        cp[i] = ahead

    def at(i):
        return i + p * (nh - 1 - 2 * i)

    stay.wait()
    swap.wait_recv()

    def mid1(f):
        return remote(fb.at[at(nh - 1), f], mr.at[f], m1_s.at[f], m1_r.at[f], t, cross)

    def mid2(f):
        return remote(db.at[nh - 1, f], mr2.at[f], m2_s.at[f], m2_r.at[f], t, cross)

    def up(f):
        return remote(et.at[f], hb.at[f], up_s.at[f], up_r.at[f], t - 1, l)

    def down(f):
        return remote(eb.at[f], ht.at[f], dn_s.at[f], dn_r.at[f], t + 1, l)

    ghost_up = remote(gs.at[0], gb, gu_s, gu_r, t - 1, l)
    ghost_down = remote(gs.at[1], gt, gd_s, gd_r, t + 1, l)

    def forward1(f, carry):
        d = None
        for i in range(nh):
            d_new = fb[at(i), f] * ip[i]
            d = d_new if d is None else d_new + gg[i] * d
            fb[at(i), f] = d
        mid1(f).start()
        return carry

    lax.fori_loop(0, nf // 2, forward1, 0)

    def mark(r, row):
        low = row.astype(jnp.int32) % LANES
        groups = lax.broadcasted_iota(jnp.int32, (LANES, width), 0)
        oh[r] = (groups == low).astype(F32).astype(jnp.bfloat16)

    def label_row(r):
        return jnp.concatenate([wl[q, 1, r : r + 1, :] for q in range(blocks)], axis=1)

    for number in range(3, 6):
        coefs_arrival(number, True).wait_recv()
    for copy in tags:
        copy.wait_recv()
    weight = jnp.concatenate([wl[q, 0] for q in range(blocks)], axis=1)
    factor = weight * hh[...]
    far = None
    for inverse, scaled, ahead in pivots(1 - p):
        far = inverse if far is None else far * scaled
    unit = None
    for i in range(nh):
        unit = ip[i] * lower if unit is None else gg[i] * unit
        mw[i] = unit
    middle = cp[nh - 1]
    inverse = 1.0 / (1.0 - middle * ahead)
    den[...] = inverse
    m = (unit + middle * (far * (1.0 - lower))) * inverse
    for i in range(nh - 1, -1, -1):
        if i < nh - 1:
            m = mw[i] + cp[i] * m
        mi = m * factor
        mw[i] = mi
        gs[0, i : i + 1, :] = mi[0:1, :]
        gs[1, i : i + 1, :] = mi[nrows - 1 : nrows, :]
    gs[0, nh : nh + 1, :] = label_row(0)
    gs[1, nh : nh + 1, :] = label_row(nrows - 1)

    @pl.when(t > 0)
    def _():
        ghost_up.start()

    @pl.when(t < tiles - 1)
    def _():
        ghost_down.start()

    lax.fori_loop(nf // 2, nf, forward1, 0)

    for r in range(nrows):
        mark(r, label_row(r))

    shape = (nrows, width)
    rows = lax.broadcasted_iota(jnp.int32, shape, 0)
    columns = lax.broadcasted_iota(jnp.int32, shape, 1)

    def backward1(f, carry):
        mid1(f).wait()
        v = None
        total = None
        for i in range(nh - 1, -1, -1):
            if v is None:
                v = (fb[at(i), f] + cp[i] * mr[f]) * den[...]
            else:
                v = fb[at(i), f] + cp[i] * v
            fb[at(i), f] = v
            et[f, i : i + 1, :] = v[0:1, :]
            eb[f, i : i + 1, :] = v[nrows - 1 : nrows, :]
            above = jnp.where(rows == 0, 0.0, pltpu.roll(v, 1, axis=0))
            below = jnp.where(rows == nrows - 1, 0.0, pltpu.roll(v, nrows - 1, axis=0))
            left = jnp.where(columns == 0, 0.0, pltpu.roll(v, 1, axis=1))
            right = jnp.where(columns == width - 1, 0.0, pltpu.roll(v, width - 1, axis=1))
            near = (above + below) + (left + right)
            db[i, f] = near
            total = mw[i] * near if total is None else total + mw[i] * near

        @pl.when(z > 0)
        def _():
            up(f).start()

        @pl.when(z < nz - 1)
        def _():
            down(f).start()

        va[f] = total + (weight * lower) * v
        return carry

    lax.fori_loop(0, nf, backward1, 0)

    for f in range(nf):
        v = va[f]
        for r in range(nrows):
            zz[r, f : f + 1, :] = v[r : r + 1, :]

    @pl.when(t > 0)
    def _():
        ghost_down.wait_recv()

    @pl.when(t < tiles - 1)
    def _():
        ghost_up.wait_recv()

    mark(nrows, gt[nh : nh + 1, :])
    mark(nrows + 1, gb[nh : nh + 1, :])
    for f in range(nf):
        zz[nrows, f : f + 1, :] = jnp.sum(gt[0:nh, :] * et[f], axis=0, keepdims=True)
        zz[nrows + 1, f : f + 1, :] = jnp.sum(gb[0:nh, :] * eb[f], axis=0, keepdims=True)
    total = jnp.zeros((12 * nf, LANES), F32)
    for r in range(nrows + 2):
        if r < nrows:
            row = label_row(r)
        else:
            row = (gt if r == nrows else gb)[nh : nh + 1, :]
        high = row.astype(jnp.int32) // LANES
        v = zz[r]
        apart = jnp.concatenate([jnp.where(high == g, v, 0.0) for g in range(4)], axis=0)
        a0 = apart.astype(jnp.bfloat16)
        rest = apart - a0.astype(F32)
        a1 = rest.astype(jnp.bfloat16)
        a2 = (rest - a1.astype(F32)).astype(jnp.bfloat16)
        total += lax.dot_general(
            jnp.concatenate([a0, a1, a2], axis=0), oh[r],
            (((1,), (1,)), ((), ())), preferred_element_type=F32,
        )
    n = 4 * nf
    sums = (total[2 * n :] + total[n : 2 * n]) + total[:n]
    for g in range(4):
        part[g] = sums[g * nf : (g + 1) * nf]

    s1[x] = part[x]
    stage1 = []
    for d in range(1, 4):
        there = (x + d) % 4
        tile, layer = at_x(there)
        stage1.append(
            remote(part.at[there], s1.at[x], r_s.at[0, d - 1], r_r.at[0, d - 1], tile, layer + c)
        )
    for copy in stage1:
        copy.start()

    @pl.when(first)
    def _():
        lax.fori_loop(0, nf, lambda f, k: (up(f).start(), k)[1], 0)

    @pl.when(last)
    def _():
        lax.fori_loop(0, nf, lambda f, k: (down(f).start(), k)[1], 0)

    def exchange(number, buffer, size, mine, stride):
        return [
            remote(buffer.at[mine], buffer.at[mine], r_s.at[number, d - 1], r_r.at[number, d - 1],
                   t + stride * ((mine + d) % size - mine), l)
            for d in range(1, size)
        ]

    stage2 = exchange(1, s2, nz, z, 1)
    stage3 = exchange(2, s3, ny, y, 2 * nz)

    def gathers():
        copies = []
        for d in range(4):
            tile, layer = at_x((x + d) % 4)
            for dc in range(2):
                if d or dc:
                    copies.append(
                        remote(res.at[c, x], res.at[c, x], g_s.at[d, dc], g_r.at[d, dc],
                               tile, layer + (c + dc) % 2)
                    )
        return copies

    def forward2(f, carry):
        @pl.when(t > 0)
        def _():
            down(f).wait_recv()

        @pl.when(t < tiles - 1)
        def _():
            up(f).wait_recv()

        d = None
        for i in range(nh):
            near = db[i, f] + jnp.where(rows == 0, ht[f, i : i + 1, :], 0.0)
            near = near + jnp.where(rows == nrows - 1, hb[f, i : i + 1, :], 0.0)
            d_new = (hh[...] * near) * ip[i]
            d = d_new if d is None else d_new + gg[i] * d
            db[i, f] = d
        mid2(f).start()
        return carry

    def give(f):
        return remote(
            fb.at[pl.ds((1 - c) * half, half), f], out.at[:, c * nf + f],
            o_s.at[f], o_r.at[f], t, partner,
        )

    def keep(f):
        return pltpu.make_async_copy(
            fb.at[pl.ds(c * half, half), f], out.at[:, c * nf + f], ol.at[f]
        )

    def backward2(f, carry):
        mid2(f).wait()
        v = None
        for i in range(nh - 1, -1, -1):
            if v is None:
                v = (db[i, f] + cp[i] * mr2[f]) * den[...]
            else:
                v = db[i, f] + cp[i] * v
            fb[at(i), f] = fb[at(i), f] + v
        give(f).start()
        keep(f).start()
        return carry

    for copy in stage1:
        copy.wait()
    s2[z] = (s1[0] + s1[1]) + (s1[2] + s1[3])
    for copy in stage2:
        copy.start()

    @pl.when(inner_tile)
    def _():
        lax.fori_loop(0, nf, forward2, 0)

    def folded(buffer, size):
        value = buffer[0]
        for k in range(1, size):
            value = value + buffer[k]
        return value

    for copy in stage2:
        copy.wait()
    s3[y] = folded(s2, nz)
    for copy in stage3:
        copy.start()

    @pl.when(jnp.logical_not(inner_tile))
    def _():
        lax.fori_loop(0, nf, forward2, 0)

    for copy in stage3:
        copy.wait()
    res[c, x] = folded(s3, ny) * scale
    for copy in gathers():
        copy.start()

    lax.fori_loop(0, nf, backward2, 0)

    for d in range(4):
        for dc in range(2):
            if d or dc:
                source = res.at[(c + dc) % 2, (x - d + 4) % 4]
                remote(source, source, g_s.at[d, dc], g_r.at[d, dc], t, partner).wait_recv()
    for core in range(2):
        for g in range(4):
            sens[core * nf : (core + 1) * nf, g * LANES : (g + 1) * LANES] = res[core, g]

    for copy in spread + spread_late + tags + [swap] + gathers():
        copy.wait_send()

    @pl.when(t > 0)
    def _():
        ghost_up.wait_send()

    @pl.when(t < tiles - 1)
    def _():
        ghost_down.wait_send()

    def drain(f, carry):
        @pl.when(t > 0)
        def _():
            up(f).wait_send()

        @pl.when(t < tiles - 1)
        def _():
            down(f).wait_send()

        keep(f).wait()
        give(f).wait()
        return carry

    lax.fori_loop(0, nf, drain, 0)


def shards(forcing, vert_coupling, horiz_coupling, basal_velocity, group_label, ice_mask):
    tiles = lax.axis_size("tile")
    layers, functionals, rows, width = forcing.shape
    nf = functionals // 2
    nh = 2 * layers
    nl = 4 * layers
    nz = min(8, tiles // 2)
    ny = tiles // (2 * nz)
    scale = -((tiles * rows * width / GROUPS) ** (-0.5))
    dma = pltpu.SemaphoreType.DMA
    vmem = pltpu.VMEM
    field = vmem((nh, nf, rows, width), F32)
    per_f = vmem((nf, rows, width), F32)
    per_layer = vmem((nh, rows, width), F32)
    flat = vmem((rows, width), F32)
    tile = vmem((rows, LANES), F32)
    whole = vmem((rows, LANES), jnp.int32)
    edge = vmem((nf, nh, width), F32)
    ghost = vmem((nh + 1, width), F32)
    pieces = vmem((4, nf, LANES), F32)
    scratch = [
        tile, flat, tile, whole, whole,
        vmem((2, rows, LANES), F32), vmem((4, nl, rows, LANES), F32), vmem((4, 2, rows, LANES), F32),
        field, field, per_f, per_layer, per_layer, per_layer, per_layer,
        flat, per_f, per_f,
        edge, edge, edge, edge, vmem((2, nh + 1, width), F32), ghost, ghost,
        vmem((rows + 2, nf, width), F32), vmem((rows + 2, LANES, width), jnp.bfloat16),
        pieces, pieces, vmem((nz, nf, LANES), F32), vmem((ny, nf, LANES), F32),
        vmem((2, 4, nf, LANES), F32),
        dma((7,)), dma((2,)), dma((6,)), dma((6,)), dma((3,)), dma((3,)),
        dma((nf,)), dma((nf,)), dma((nf,)), dma((nf,)),
        dma((nf,)), dma((nf,)), dma((nf,)), dma((nf,)),
        dma, dma, dma, dma,
        dma((nf,)), dma((nf,)), dma((nf,)),
        dma((3, 8)), dma((3, 8)), dma((4, 2)), dma((4, 2)),
    ]
    operands = (forcing, vert_coupling, horiz_coupling, basal_velocity, group_label, ice_mask)
    return pl.pallas_call(
        functools.partial(kernel, tiles, scale),
        out_shape=(
            jax.ShapeDtypeStruct(forcing.shape, F32),
            jax.ShapeDtypeStruct((functionals, GROUPS), F32),
        ),
        in_specs=[pl.BlockSpec(memory_space=pltpu.HBM)] * 6,
        out_specs=(pl.BlockSpec(memory_space=pl.ANY), pl.BlockSpec(memory_space=pltpu.VMEM)),
        scratch_shapes=scratch,
        compiler_params=pltpu.CompilerParams(
            collective_id=0, has_side_effects=True, vmem_limit_bytes=32 * 1024 * 1024
        ),
        name="sweeps",
    )(*[pltpu.with_memory_space_constraint(operand, pltpu.HBM) for operand in operands])


def solution(mesh):
    in_specs = (
        P("layer", None, "tile", None),
        P(None, "tile", "layer"),
        P("tile", None),
        P("tile", "layer"),
        P("tile", "layer"),
        P("tile", "layer"),
    )
    out_specs = (P("layer", None, "tile", None), P())
    return jax.shard_map(shards, mesh=mesh, in_specs=in_specs, out_specs=out_specs, check_vma=False)
```

```python
import functools

import jax
import jax.numpy as jnp
from jax import lax
from jax.experimental import pallas as pl
from jax.experimental.pallas import tpu as pltpu
from jax.sharding import PartitionSpec as P

GROUPS = 512
LANES = 128
MESH = pl.DeviceIdType.MESH
F32 = jnp.float32


def kernel(
    tiles, scale,
    forc, vert, horiz, basal, label, mask,
    out, sens,
    v0, hh, bb, ll, mm, pack, vb, wl, fb, db, va, ip, gg, cp, mw, cpo, mwo, gam, rw, er, den, mr, mr2,
    et, eb, ht, hb, gs, gt, gb, zz, oh, part, s1, s2, res,
    lsem, fsem, c_s, c_r, w_s, w_r, m1_s, m1_r, m2_s, m2_r,
    up_s, up_r, dn_s, dn_r, gu_s, gu_r, gd_s, gd_r, o_s, o_r, ol, r_s, r_r, g_s, g_r, hello,
):
    nf = fb.shape[1]
    nh = fb.shape[0]
    half = nh // 2
    nrows, width = hh.shape
    blocks = width // LANES
    nz = min(8, tiles // 2)
    ny = tiles // (2 * nz)
    t = lax.axis_index("tile")
    l = lax.axis_index("layer")
    p = l // 2
    c = l - 2 * p
    z = t % nz
    x = 2 * ((t // nz) % 2) + p
    y = t // (2 * nz)
    partner = 2 * p + 1 - c
    cross = 2 * (1 - p) + c
    diag = 2 * (1 - p) + 1 - c

    def at_x(number):
        return t + nz * (number // 2 - (x // 2)), 2 * (number % 2)

    def remote(src, dst, ssem, rsem, tile, layer):
        return pltpu.make_async_remote_copy(
            src_ref=src, dst_ref=dst, send_sem=ssem, recv_sem=rsem,
            device_id=(tile, layer), device_id_type=MESH,
        )

    barrier = pltpu.get_barrier_semaphore()
    first = jnp.logical_and(z == 0, t > 0)
    last = jnp.logical_and(z == nz - 1, t < tiles - 1)
    beside, side_layer = at_x((x + 3 + 2 * (x % 2)) % 4)
    near = [
        (t, cross), (t, diag), (t, partner), (beside, side_layer + c),
        (t - z + (z + 1) % nz, l), (t - z + (z + nz - 1) % nz, l),
    ]
    if ny > 1:
        near.append((t + 2 * nz * ((y + 1) % ny - y), l))
        near.append((t + 2 * nz * ((y + ny - 1) % ny - y), l))

    def tell_near(semaphore):
        for tile, layer in near:
            pl.semaphore_signal(
                semaphore, inc=1, device_id=(tile, layer), device_id_type=MESH
            )

    tell_near(barrier)

    local = [
        pltpu.make_async_copy(vert.at[0], v0, lsem.at[0]),
        pltpu.make_async_copy(horiz, hh, lsem.at[1]),
        pltpu.make_async_copy(basal, bb, lsem.at[2]),
        pltpu.make_async_copy(label, ll, lsem.at[3]),
        pltpu.make_async_copy(mask, mm, lsem.at[4]),
    ]
    for copy in local:
        copy.start()
    own = pltpu.make_async_copy(vert, vb.at[l], lsem.at[5])
    own.start()
    stay = pltpu.make_async_copy(
        forc.at[:, pl.ds(c * nf, nf)], fb.at[pl.ds(c * half, half)], lsem.at[6]
    )
    stay.start()

    pl.semaphore_wait(barrier, len(near))

    spread = [
        remote(vert, vb.at[l], c_s.at[k], c_r.at[k], t, layer)
        for k, layer in enumerate((cross, diag, partner))
    ]
    for copy in spread:
        copy.start()
    tell_near(hello.at[0])
    swap = remote(
        forc.at[:, pl.ds((1 - c) * nf, nf)], fb.at[pl.ds(c * half, half)],
        fsem.at[0], fsem.at[1], t, partner,
    )

    for copy in local:
        copy.wait()
    pack[0] = v0[...] * bb[...] * mm[...].astype(F32)
    pack[1] = ll[...].astype(F32)
    tags = [
        remote(pack, wl.at[l], w_s.at[k], w_r.at[k], t, layer)
        for k, layer in enumerate((cross, diag, partner))
    ]
    for copy in tags:
        copy.start()
    swap.start()

    for k in range(2):
        pl.semaphore_wait(hello.at[k], len(near))
        tell_near(hello.at[k + 1])
    wl[l] = pack[...]

    @pl.when(t == 0)
    def _():
        ht[...] = jnp.zeros_like(ht)
        gt[...] = jnp.zeros_like(gt)

    @pl.when(t == tiles - 1)
    def _():
        hb[...] = jnp.zeros_like(hb)
        gb[...] = jnp.zeros_like(gb)

    own.wait()
    for copy in spread:
        copy.wait_recv()

    h4 = 4.0 * hh[...]

    def coupling(i, chip):
        value = jnp.concatenate(
            [vb[q, (i if i else 15 * chip) + chip * (16 - 2 * i if i else 0)] for q in range(blocks)],
            axis=1,
        )
        return value if i else value * (1 - chip).astype(F32)

    def pivots(chip):
        outer = coupling(0, chip)
        prev = None
        for i in range(nh):
            inner = coupling(i + 1, chip)
            pivot = outer + inner + h4
            if prev is not None:
                pivot = pivot - outer * prev
            inverse = 1.0 / pivot
            prev = inner * inverse
            yield inverse, outer * inverse, prev
            outer = inner

    lower = (1 - p).astype(F32)
    for i, (inverse, scaled, ahead) in enumerate(pivots(p)):
        ip[i] = inverse
        gg[i] = scaled
        cp[i] = ahead

    def at(i):
        return i + p * (nh - 1 - 2 * i)

    def mid1(f):
        return remote(fb.at[at(nh - 1), f], mr.at[f], m1_s.at[f], m1_r.at[f], t, cross)

    def mid2(f):
        return remote(db.at[nh - 1, f], mr2.at[f], m2_s.at[f], m2_r.at[f], t, cross)

    def up(f):
        return remote(et.at[f], hb.at[f], up_s.at[f], up_r.at[f], t - 1, l)

    def down(f):
        return remote(eb.at[f], ht.at[f], dn_s.at[f], dn_r.at[f], t + 1, l)

    ghost_up = remote(gs.at[0], gb, gu_s, gu_r, t - 1, l)
    ghost_down = remote(gs.at[1], gt, gd_s, gd_r, t + 1, l)

    def forward1(f, carry):
        d = None
        for i in range(nh):
            d_new = fb[at(i), f] * ip[i]
            d = d_new if d is None else d_new + gg[i] * d
            fb[at(i), f] = d
        mid1(f).start()
        return carry


    def mark(r, row):
        low = row.astype(jnp.int32) % LANES
        groups = lax.broadcasted_iota(jnp.int32, (LANES, width), 0)
        oh[r] = (groups == low).astype(F32).astype(jnp.bfloat16)

    def label_row(r):
        return jnp.concatenate([wl[q, 1, r : r + 1, :] for q in range(blocks)], axis=1)

    for copy in tags:
        copy.wait_recv()
    weight = jnp.concatenate([wl[q, 0] for q in range(blocks)], axis=1)
    factor = weight * hh[...]
    upper = 1.0 - lower
    for i, (inverse, scaled, ahead) in enumerate(pivots(1 - p)):
        far = inverse * upper if i == 0 else scaled * far
        mwo[i] = far
        cpo[i] = ahead
    unit = None
    for i in range(nh):
        unit = ip[i] * lower if unit is None else gg[i] * unit
        mw[i] = unit
    middle = cp[nh - 1]
    inverse = 1.0 / (1.0 - middle * ahead)
    den[...] = inverse
    m = (unit + middle * far) * inverse
    mo = (far + ahead * unit) * inverse
    reach = ahead
    shape = (nrows, width)
    rows = lax.broadcasted_iota(jnp.int32, shape, 0)
    columns = lax.broadcasted_iota(jnp.int32, shape, 1)

    def neighbours(v):
        return (
            jnp.where(rows == 0, 0.0, pltpu.roll(v, 1, axis=0)),
            jnp.where(rows == nrows - 1, 0.0, pltpu.roll(v, nrows - 1, axis=0)),
            jnp.where(columns == 0, 0.0, pltpu.roll(v, 1, axis=1)),
            jnp.where(columns == width - 1, 0.0, pltpu.roll(v, width - 1, axis=1)),
        )

    across = None
    for i in range(nh - 1, -1, -1):
        if i < nh - 1:
            m = mw[i] + cp[i] * m
            mo = mwo[i] + cpo[i] * mo
            reach = cpo[i] * reach
        mi = m * factor
        moi = mo * factor
        mw[i] = mi
        for side, row in ((0, 0), (1, nrows - 1)):
            gs[side, i : i + 1, :] = mi[row : row + 1, :]
            gs[side, nh + i : nh + i + 1, :] = moi[row : row + 1, :]
            er[side, i : i + 1, :] = reach[row : row + 1, :]
        terms = [moi * v for v in neighbours(reach)]
        across = terms if across is None else [v + w for v, w in zip(across, terms)]
    for k in range(4):
        gam[k] = across[k]
    rw[...] = reach * (weight * upper)
    gs[0, 2 * nh : 2 * nh + 1, :] = label_row(0)
    gs[1, 2 * nh : 2 * nh + 1, :] = label_row(nrows - 1)

    pl.semaphore_wait(hello.at[2], len(near))

    @pl.when(t > 0)
    def _():
        ghost_up.start()

    @pl.when(t < tiles - 1)
    def _():
        ghost_down.start()

    stay.wait()
    swap.wait_recv()
    lax.fori_loop(0, nf, forward1, 0)

    def bed(f, carry):
        v = None
        total = None
        for i in range(nh - 1, -1, -1):
            if v is None:
                v = fb[at(i), f] * den[...]
                parts = neighbours(v)
                total = rw[...] * v
                for k in range(4):
                    total = total + gam[k] * parts[k]
            else:
                v = fb[at(i), f] + cp[i] * v
                parts = neighbours(v)
            total = total + mw[i] * ((parts[0] + parts[1]) + (parts[2] + parts[3]))
            et[f, i : i + 1, :] = v[0:1, :]
            eb[f, i : i + 1, :] = v[nrows - 1 : nrows, :]
        va[f] = total + (weight * lower) * v
        return carry

    lax.fori_loop(0, nf, bed, 0)

    for r in range(nrows):
        mark(r, label_row(r))

    for f in range(nf):
        v = va[f]
        for r in range(nrows):
            zz[r, f : f + 1, :] = v[r : r + 1, :]

    @pl.when(t > 0)
    def _():
        ghost_down.wait_recv()

    @pl.when(t < tiles - 1)
    def _():
        ghost_up.wait_recv()

    mark(nrows, gt[2 * nh : 2 * nh + 1, :])
    mark(nrows + 1, gb[2 * nh : 2 * nh + 1, :])
    beyond_up = jnp.sum(gt[nh : 2 * nh, :] * er[0], axis=0, keepdims=True)
    beyond_down = jnp.sum(gb[nh : 2 * nh, :] * er[1], axis=0, keepdims=True)
    for f in range(nf):
        first_row = jnp.sum(gt[0:nh, :] * et[f], axis=0, keepdims=True)
        last_row = jnp.sum(gb[0:nh, :] * eb[f], axis=0, keepdims=True)
        zz[nrows, f : f + 1, :] = first_row + beyond_up * et[f, nh - 1 : nh, :]
        zz[nrows + 1, f : f + 1, :] = last_row + beyond_down * eb[f, nh - 1 : nh, :]
    total = jnp.zeros((12 * nf, LANES), F32)
    for r in range(nrows + 2):
        if r < nrows:
            row = label_row(r)
        else:
            row = (gt if r == nrows else gb)[2 * nh : 2 * nh + 1, :]
        high = row.astype(jnp.int32) // LANES
        v = zz[r]
        apart = jnp.concatenate([jnp.where(high == g, v, 0.0) for g in range(4)], axis=0)
        a0 = apart.astype(jnp.bfloat16)
        rest = apart - a0.astype(F32)
        a1 = rest.astype(jnp.bfloat16)
        a2 = (rest - a1.astype(F32)).astype(jnp.bfloat16)
        total += lax.dot_general(
            jnp.concatenate([a0, a1, a2], axis=0), oh[r],
            (((1,), (1,)), ((), ())), preferred_element_type=F32,
        )
    n = 4 * nf
    sums = (total[2 * n :] + total[n : 2 * n]) + total[:n]
    for g in range(4):
        part[g] = sums[g * nf : (g + 1) * nf]

    place = 4 * y + x
    s1[place] = part[x]
    stage1 = []
    for e in range(ny):
        for d in range(4):
            if d or e:
                there = (x + d) % 4
                tile, layer = at_x(there)
                tile = tile + 2 * nz * ((y + e) % ny - y)
                stage1.append(
                    remote(part.at[there], s1.at[place], r_s.at[0, 4 * e + d],
                           r_r.at[0, 4 * e + d], tile, layer + c)
                )
    for copy in stage1:
        copy.start()

    def backward1(f, carry):
        mid1(f).wait()
        v = None
        for i in range(nh - 1, -1, -1):
            if v is None:
                v = (fb[at(i), f] + cp[i] * mr[f]) * den[...]
            else:
                v = fb[at(i), f] + cp[i] * v
            fb[at(i), f] = v
            et[f, i : i + 1, :] = v[0:1, :]
            eb[f, i : i + 1, :] = v[nrows - 1 : nrows, :]
            parts = neighbours(v)
            db[i, f] = (parts[0] + parts[1]) + (parts[2] + parts[3])

        @pl.when(z > 0)
        def _():
            up(f).start()

        @pl.when(z < nz - 1)
        def _():
            down(f).start()

        return carry

    lax.fori_loop(0, nf, backward1, 0)

    @pl.when(first)
    def _():
        lax.fori_loop(0, nf, lambda f, k: (up(f).start(), k)[1], 0)

    @pl.when(last)
    def _():
        lax.fori_loop(0, nf, lambda f, k: (down(f).start(), k)[1], 0)

    def exchange(number, buffer, size, mine, stride):
        return [
            remote(buffer.at[mine], buffer.at[mine], r_s.at[number, d - 1], r_r.at[number, d - 1],
                   t + stride * ((mine + d) % size - mine), l)
            for d in range(1, size)
        ]

    stage2 = exchange(1, s2, nz, z, 1)

    def gathers():
        copies = []
        for d in range(4):
            tile, layer = at_x((x + d) % 4)
            for dc in range(2):
                if d or dc:
                    copies.append(
                        remote(res.at[c, x], res.at[c, x], g_s.at[d, dc], g_r.at[d, dc],
                               tile, layer + (c + dc) % 2)
                    )
        return copies

    def forward2(f, carry):
        @pl.when(t > 0)
        def _():
            down(f).wait_recv()

        @pl.when(t < tiles - 1)
        def _():
            up(f).wait_recv()

        d = None
        for i in range(nh):
            near = db[i, f] + jnp.where(rows == 0, ht[f, i : i + 1, :], 0.0)
            near = near + jnp.where(rows == nrows - 1, hb[f, i : i + 1, :], 0.0)
            d_new = (hh[...] * near) * ip[i]
            d = d_new if d is None else d_new + gg[i] * d
            db[i, f] = d
        mid2(f).start()
        return carry

    def give(f):
        return remote(
            fb.at[pl.ds((1 - c) * half, half), f], out.at[:, c * nf + f],
            o_s.at[f], o_r.at[f], t, partner,
        )

    def keep(f):
        return pltpu.make_async_copy(
            fb.at[pl.ds(c * half, half), f], out.at[:, c * nf + f], ol.at[f]
        )

    def backward2(f, carry):
        mid2(f).wait()
        v = None
        for i in range(nh - 1, -1, -1):
            if v is None:
                v = (db[i, f] + cp[i] * mr2[f]) * den[...]
            else:
                v = db[i, f] + cp[i] * v
            fb[at(i), f] = fb[at(i), f] + v
        give(f).start()
        keep(f).start()
        return carry

    def folded(buffer, size):
        value = buffer[0]
        for k in range(1, size):
            value = value + buffer[k]
        return value

    for copy in stage1:
        copy.wait()
    s2[z] = folded(s1, 4 * ny)
    for copy in stage2:
        copy.start()

    lax.fori_loop(0, nf, forward2, 0)

    for copy in stage2:
        copy.wait()
    res[c, x] = folded(s2, nz) * scale
    for copy in gathers():
        copy.start()

    lax.fori_loop(0, nf, backward2, 0)

    for d in range(4):
        for dc in range(2):
            if d or dc:
                source = res.at[(c + dc) % 2, (x - d + 4) % 4]
                remote(source, source, g_s.at[d, dc], g_r.at[d, dc], t, partner).wait_recv()
    for core in range(2):
        for g in range(4):
            sens[core * nf : (core + 1) * nf, g * LANES : (g + 1) * LANES] = res[core, g]

    for copy in spread + tags + [swap] + gathers():
        copy.wait_send()

    @pl.when(t > 0)
    def _():
        ghost_up.wait_send()

    @pl.when(t < tiles - 1)
    def _():
        ghost_down.wait_send()

    def drain(f, carry):
        @pl.when(t > 0)
        def _():
            up(f).wait_send()

        @pl.when(t < tiles - 1)
        def _():
            down(f).wait_send()

        keep(f).wait()
        give(f).wait()
        return carry

    lax.fori_loop(0, nf, drain, 0)


def shards(forcing, vert_coupling, horiz_coupling, basal_velocity, group_label, ice_mask):
    tiles = lax.axis_size("tile")
    layers, functionals, rows, width = forcing.shape
    nf = functionals // 2
    nh = 2 * layers
    nl = 4 * layers
    nz = min(8, tiles // 2)
    ny = tiles // (2 * nz)
    scale = -((tiles * rows * width / GROUPS) ** (-0.5))
    dma = pltpu.SemaphoreType.DMA
    vmem = pltpu.VMEM
    field = vmem((nh, nf, rows, width), F32)
    per_f = vmem((nf, rows, width), F32)
    per_layer = vmem((nh, rows, width), F32)
    flat = vmem((rows, width), F32)
    tile = vmem((rows, LANES), F32)
    whole = vmem((rows, LANES), jnp.int32)
    edge = vmem((nf, nh, width), F32)
    ghost = vmem((2 * nh + 1, width), F32)
    pieces = vmem((4, nf, LANES), F32)
    scratch = [
        tile, flat, tile, whole, whole,
        vmem((2, rows, LANES), F32), vmem((4, nl, rows, LANES), F32), vmem((4, 2, rows, LANES), F32),
        field, field, per_f, per_layer, per_layer, per_layer, per_layer,
        per_layer, per_layer, vmem((4, rows, width), F32), flat, vmem((2, nh, width), F32),
        flat, per_f, per_f,
        edge, edge, edge, edge, vmem((2, 2 * nh + 1, width), F32), ghost, ghost,
        vmem((rows + 2, nf, width), F32), vmem((rows + 2, LANES, width), jnp.bfloat16),
        pieces, vmem((4 * ny, nf, LANES), F32), vmem((nz, nf, LANES), F32),
        vmem((2, 4, nf, LANES), F32),
        dma((7,)), dma((2,)), dma((3,)), dma((3,)), dma((3,)), dma((3,)),
        dma((nf,)), dma((nf,)), dma((nf,)), dma((nf,)),
        dma((nf,)), dma((nf,)), dma((nf,)), dma((nf,)),
        dma, dma, dma, dma,
        dma((nf,)), dma((nf,)), dma((nf,)),
        dma((2, 16)), dma((2, 16)), dma((4, 2)), dma((4, 2)), pltpu.SemaphoreType.REGULAR((3,)),
    ]
    operands = (forcing, vert_coupling, horiz_coupling, basal_velocity, group_label, ice_mask)
    return pl.pallas_call(
        functools.partial(kernel, tiles, scale),
        out_shape=(
            jax.ShapeDtypeStruct(forcing.shape, F32),
            jax.ShapeDtypeStruct((functionals, GROUPS), F32),
        ),
        in_specs=[pl.BlockSpec(memory_space=pltpu.HBM)] * 6,
        out_specs=(pl.BlockSpec(memory_space=pl.ANY), pl.BlockSpec(memory_space=pltpu.VMEM)),
        scratch_shapes=scratch,
        compiler_params=pltpu.CompilerParams(
            collective_id=0, has_side_effects=True, vmem_limit_bytes=32 * 1024 * 1024
        ),
        name="sweeps",
    )(*[pltpu.with_memory_space_constraint(operand, pltpu.HBM) for operand in operands])


def solution(mesh):
    in_specs = (
        P("layer", None, "tile", None),
        P(None, "tile", "layer"),
        P("tile", None),
        P("tile", "layer"),
        P("tile", "layer"),
        P("tile", "layer"),
    )
    out_specs = (P("layer", None, "tile", None), P())
    return jax.shard_map(shards, mesh=mesh, in_specs=in_specs, out_specs=out_specs, check_vma=False)
```

```python
import functools

import jax
import jax.numpy as jnp
from jax import lax
from jax.experimental import pallas as pl
from jax.experimental.pallas import tpu as pltpu
from jax.sharding import PartitionSpec as P

GROUPS = 512
LANES = 128
MESH = pl.DeviceIdType.MESH
F32 = jnp.float32


def farthest_first(steps, sizes):
    def hops(step):
        return sum(min(k, size - k) for k, size in zip(step, sizes))

    return sorted((step for step in steps if hops(step)), key=hops, reverse=True)


def kernel(
    tiles, scale,
    forc, vert, horiz, basal, label, mask,
    out, sens,
    v0, hh, bb, ll, mm, pack, vb, wl, fb, db, va, ip, gg, cp, mw, cpo, mwo, gam, rw, er, den, mr, mr2,
    et, eb, ht, hb, gs, gt, gb, zz, oh, part, s1, s2, res,
    lsem, fsem, c_s, c_r, w_s, w_r, m1_s, m1_r, m2_s, m2_r,
    up_s, up_r, dn_s, dn_r, gu_s, gu_r, gd_s, gd_r, o_s, o_r, ol, r_s, r_r, g_s, g_r, hello,
):
    nf = fb.shape[1]
    nh = fb.shape[0]
    half = nh // 2
    nrows, width = hh.shape
    blocks = width // LANES
    nz = min(8, tiles // 2)
    ny = tiles // (2 * nz)
    t = lax.axis_index("tile")
    l = lax.axis_index("layer")
    p = l // 2
    c = l - 2 * p
    z = t % nz
    x = 2 * ((t // nz) % 2) + p
    y = t // (2 * nz)
    partner = 2 * p + 1 - c
    cross = 2 * (1 - p) + c
    diag = 2 * (1 - p) + 1 - c

    def at_x(number):
        return t + nz * (number // 2 - (x // 2)), 2 * (number % 2)

    def remote(src, dst, ssem, rsem, tile, layer):
        return pltpu.make_async_remote_copy(
            src_ref=src, dst_ref=dst, send_sem=ssem, recv_sem=rsem,
            device_id=(tile, layer), device_id_type=MESH,
        )

    barrier = pltpu.get_barrier_semaphore()
    first = jnp.logical_and(z == 0, t > 0)
    last = jnp.logical_and(z == nz - 1, t < tiles - 1)
    beside, side_layer = at_x((x + 3 + 2 * (x % 2)) % 4)
    near = [
        (t, cross), (t, diag), (t, partner), (beside, side_layer + c),
        (t - z + (z + 1) % nz, l), (t - z + (z + nz - 1) % nz, l),
    ]
    if ny > 1:
        near.append((t + 2 * nz * ((y + 1) % ny - y), l))
        near.append((t + 2 * nz * ((y + ny - 1) % ny - y), l))

    def tell_near(semaphore):
        for tile, layer in near:
            pl.semaphore_signal(
                semaphore, inc=1, device_id=(tile, layer), device_id_type=MESH
            )

    tell_near(barrier)

    local = [
        pltpu.make_async_copy(vert.at[0], v0, lsem.at[0]),
        pltpu.make_async_copy(horiz, hh, lsem.at[1]),
        pltpu.make_async_copy(basal, bb, lsem.at[2]),
        pltpu.make_async_copy(label, ll, lsem.at[3]),
        pltpu.make_async_copy(mask, mm, lsem.at[4]),
    ]
    for copy in local:
        copy.start()
    own = pltpu.make_async_copy(vert, vb.at[l], lsem.at[5])
    own.start()
    stay = pltpu.make_async_copy(
        forc.at[:, pl.ds(c * nf, nf)], fb.at[pl.ds(c * half, half)], lsem.at[6]
    )
    stay.start()

    pl.semaphore_wait(barrier, len(near))

    spread = [
        remote(vert, vb.at[l], c_s.at[k], c_r.at[k], t, layer)
        for k, layer in enumerate((cross, diag, partner))
    ]
    for copy in spread:
        copy.start()
    tell_near(hello.at[0])
    swap = remote(
        forc.at[:, pl.ds((1 - c) * nf, nf)], fb.at[pl.ds(c * half, half)],
        fsem.at[0], fsem.at[1], t, partner,
    )

    for copy in local:
        copy.wait()
    pack[0] = v0[...] * bb[...] * mm[...].astype(F32)
    pack[1] = ll[...].astype(F32)
    tags = [
        remote(pack, wl.at[l], w_s.at[k], w_r.at[k], t, layer)
        for k, layer in enumerate((cross, diag, partner))
    ]
    for copy in tags:
        copy.start()
    swap.start()

    for k in range(2):
        pl.semaphore_wait(hello.at[k], len(near))
        tell_near(hello.at[k + 1])
    wl[l] = pack[...]

    @pl.when(t == 0)
    def _():
        ht[...] = jnp.zeros_like(ht)
        gt[...] = jnp.zeros_like(gt)

    @pl.when(t == tiles - 1)
    def _():
        hb[...] = jnp.zeros_like(hb)
        gb[...] = jnp.zeros_like(gb)

    own.wait()
    for copy in spread:
        copy.wait_recv()

    h4 = 4.0 * hh[...]

    def coupling(i, chip):
        value = jnp.concatenate(
            [vb[q, (i if i else 15 * chip) + chip * (16 - 2 * i if i else 0)] for q in range(blocks)],
            axis=1,
        )
        return value if i else value * (1 - chip).astype(F32)

    def pivots(chip):
        outer = coupling(0, chip)
        prev = None
        for i in range(nh):
            inner = coupling(i + 1, chip)
            pivot = outer + inner + h4
            if prev is not None:
                pivot = pivot - outer * prev
            inverse = 1.0 / pivot
            prev = inner * inverse
            yield inverse, outer * inverse, prev
            outer = inner

    lower = (1 - p).astype(F32)
    for i, (inverse, scaled, ahead) in enumerate(pivots(p)):
        ip[i] = inverse
        gg[i] = scaled
        cp[i] = ahead

    def at(i):
        return i + p * (nh - 1 - 2 * i)

    def mid1(f):
        return remote(fb.at[at(nh - 1), f], mr.at[f], m1_s.at[f], m1_r.at[f], t, cross)

    def mid2(f):
        return remote(db.at[nh - 1, f], mr2.at[f], m2_s.at[f], m2_r.at[f], t, cross)

    def up(f):
        return remote(et.at[f], hb.at[f], up_s.at[f], up_r.at[f], t - 1, l)

    def down(f):
        return remote(eb.at[f], ht.at[f], dn_s.at[f], dn_r.at[f], t + 1, l)

    ghost_up = remote(gs.at[0], gb, gu_s, gu_r, t - 1, l)
    ghost_down = remote(gs.at[1], gt, gd_s, gd_r, t + 1, l)

    def forward1(f, carry):
        d = None
        for i in range(nh):
            d_new = fb[at(i), f] * ip[i]
            d = d_new if d is None else d_new + gg[i] * d
            fb[at(i), f] = d
        mid1(f).start()
        return carry


    def mark(r, row):
        low = row.astype(jnp.int32) % LANES
        groups = lax.broadcasted_iota(jnp.int32, (LANES, width), 0)
        oh[r] = (groups == low).astype(F32).astype(jnp.bfloat16)

    def label_row(r):
        return jnp.concatenate([wl[q, 1, r : r + 1, :] for q in range(blocks)], axis=1)

    for copy in tags:
        copy.wait_recv()
    weight = jnp.concatenate([wl[q, 0] for q in range(blocks)], axis=1)
    factor = weight * hh[...]
    upper = 1.0 - lower
    for i, (inverse, scaled, ahead) in enumerate(pivots(1 - p)):
        far = inverse * upper if i == 0 else scaled * far
        mwo[i] = far
        cpo[i] = ahead
    unit = None
    for i in range(nh):
        unit = ip[i] * lower if unit is None else gg[i] * unit
        mw[i] = unit
    middle = cp[nh - 1]
    inverse = 1.0 / (1.0 - middle * ahead)
    den[...] = inverse
    m = (unit + middle * far) * inverse
    mo = (far + ahead * unit) * inverse
    shape = (nrows, width)
    rows = lax.broadcasted_iota(jnp.int32, shape, 0)
    columns = lax.broadcasted_iota(jnp.int32, shape, 1)

    def neighbours(v):
        return (
            jnp.where(rows == 0, 0.0, pltpu.roll(v, 1, axis=0)),
            jnp.where(rows == nrows - 1, 0.0, pltpu.roll(v, nrows - 1, axis=0)),
            jnp.where(columns == 0, 0.0, pltpu.roll(v, 1, axis=1)),
            jnp.where(columns == width - 1, 0.0, pltpu.roll(v, width - 1, axis=1)),
        )

    for i in range(nh - 1, -1, -1):
        if i < nh - 1:
            m = mw[i] + cp[i] * m
            mo = mwo[i] + cpo[i] * mo
        mi = m * factor
        moi = mo * factor
        mw[i] = mi
        for side, row in ((0, 0), (1, nrows - 1)):
            gs[side, i : i + 1, :] = mi[row : row + 1, :]
            gs[side, nh + i : nh + i + 1, :] = moi[row : row + 1, :]
        mwo[i] = moi
    gs[0, 2 * nh : 2 * nh + 1, :] = label_row(0)
    gs[1, 2 * nh : 2 * nh + 1, :] = label_row(nrows - 1)

    pl.semaphore_wait(hello.at[2], len(near))

    @pl.when(t > 0)
    def _():
        ghost_up.start()

    @pl.when(t < tiles - 1)
    def _():
        ghost_down.start()

    reach = None
    across = None
    for i in range(nh - 1, -1, -1):
        reach = cpo[i] if reach is None else cpo[i] * reach
        for side, row in ((0, 0), (1, nrows - 1)):
            er[side, i : i + 1, :] = reach[row : row + 1, :]
        terms = [mwo[i] * v for v in neighbours(reach)]
        across = terms if across is None else [v + w for v, w in zip(across, terms)]
    for k in range(4):
        gam[k] = across[k]
    rw[...] = reach * (weight * upper)

    stay.wait()
    swap.wait_recv()
    lax.fori_loop(0, nf, forward1, 0)

    for r in range(nrows):
        mark(r, label_row(r))

    def bed(f, carry):
        v = None
        total = None
        for i in range(nh - 1, -1, -1):
            if v is None:
                v = fb[at(i), f] * den[...]
                parts = neighbours(v)
                total = rw[...] * v
                for k in range(4):
                    total = total + gam[k] * parts[k]
            else:
                v = fb[at(i), f] + cp[i] * v
                parts = neighbours(v)
            total = total + mw[i] * ((parts[0] + parts[1]) + (parts[2] + parts[3]))
            et[f, i : i + 1, :] = v[0:1, :]
            eb[f, i : i + 1, :] = v[nrows - 1 : nrows, :]
        va[f] = total + (weight * lower) * v
        return carry

    lax.fori_loop(0, nf, bed, 0)

    for f in range(nf):
        v = va[f]
        for r in range(nrows):
            zz[r, f : f + 1, :] = v[r : r + 1, :]

    @pl.when(t > 0)
    def _():
        ghost_down.wait_recv()

    @pl.when(t < tiles - 1)
    def _():
        ghost_up.wait_recv()

    mark(nrows, gt[2 * nh : 2 * nh + 1, :])
    mark(nrows + 1, gb[2 * nh : 2 * nh + 1, :])
    beyond_up = jnp.sum(gt[nh : 2 * nh, :] * er[0], axis=0, keepdims=True)
    beyond_down = jnp.sum(gb[nh : 2 * nh, :] * er[1], axis=0, keepdims=True)
    for f in range(nf):
        first_row = jnp.sum(gt[0:nh, :] * et[f], axis=0, keepdims=True)
        last_row = jnp.sum(gb[0:nh, :] * eb[f], axis=0, keepdims=True)
        zz[nrows, f : f + 1, :] = first_row + beyond_up * et[f, nh - 1 : nh, :]
        zz[nrows + 1, f : f + 1, :] = last_row + beyond_down * eb[f, nh - 1 : nh, :]
    total = jnp.zeros((12 * nf, LANES), F32)
    for r in range(nrows + 2):
        if r < nrows:
            row = label_row(r)
        else:
            row = (gt if r == nrows else gb)[2 * nh : 2 * nh + 1, :]
        high = row.astype(jnp.int32) // LANES
        v = zz[r]
        apart = jnp.concatenate([jnp.where(high == g, v, 0.0) for g in range(4)], axis=0)
        a0 = apart.astype(jnp.bfloat16)
        rest = apart - a0.astype(F32)
        a1 = rest.astype(jnp.bfloat16)
        a2 = (rest - a1.astype(F32)).astype(jnp.bfloat16)
        total += lax.dot_general(
            jnp.concatenate([a0, a1, a2], axis=0), oh[r],
            (((1,), (1,)), ((), ())), preferred_element_type=F32,
        )
    n = 4 * nf
    sums = (total[2 * n :] + total[n : 2 * n]) + total[:n]
    for g in range(4):
        part[g] = sums[g * nf : (g + 1) * nf]

    place = 4 * y + x
    s1[place] = part[x]
    stage1 = []
    for e, d in farthest_first([(e, d) for e in range(ny) for d in range(4)], (ny, 4)):
        there = (x + d) % 4
        tile, layer = at_x(there)
        tile = tile + 2 * nz * ((y + e) % ny - y)
        stage1.append(
            remote(part.at[there], s1.at[place], r_s.at[0, 4 * e + d],
                   r_r.at[0, 4 * e + d], tile, layer + c)
        )
    for copy in stage1:
        copy.start()

    def backward1(f, carry):
        mid1(f).wait()
        v = None
        for i in range(nh - 1, -1, -1):
            if v is None:
                v = (fb[at(i), f] + cp[i] * mr[f]) * den[...]
            else:
                v = fb[at(i), f] + cp[i] * v
            fb[at(i), f] = v
            et[f, i : i + 1, :] = v[0:1, :]
            eb[f, i : i + 1, :] = v[nrows - 1 : nrows, :]
            parts = neighbours(v)
            db[i, f] = (parts[0] + parts[1]) + (parts[2] + parts[3])

        @pl.when(z > 0)
        def _():
            up(f).start()

        @pl.when(z < nz - 1)
        def _():
            down(f).start()

        return carry

    lax.fori_loop(0, nf, backward1, 0)

    @pl.when(first)
    def _():
        lax.fori_loop(0, nf, lambda f, k: (up(f).start(), k)[1], 0)

    @pl.when(last)
    def _():
        lax.fori_loop(0, nf, lambda f, k: (down(f).start(), k)[1], 0)

    def exchange(number, buffer, size, mine, stride):
        return [
            remote(buffer.at[mine], buffer.at[mine], r_s.at[number, d - 1], r_r.at[number, d - 1],
                   t + stride * ((mine + d) % size - mine), l)
            for (d,) in farthest_first([(d,) for d in range(size)], (size,))
        ]

    stage2 = exchange(1, s2, nz, z, 1)

    def slot(core, number):
        return sens.at[
            pl.ds(pl.multiple_of(core * nf, nf), nf),
            pl.ds(pl.multiple_of(number * LANES, LANES), LANES),
        ]

    own_sum = pltpu.make_async_copy(res, slot(c, x), lsem.at[4])

    def gathers():
        copies = []
        for d, dc in farthest_first([(d, dc) for d in range(4) for dc in range(2)], (4, 2)):
            tile, layer = at_x((x + d) % 4)
            copies.append(
                remote(res, slot(c, x), g_s.at[d, dc], g_r.at[d, dc],
                       tile, layer + (c + dc) % 2)
            )
        return copies

    def forward2(f, carry):
        @pl.when(t > 0)
        def _():
            down(f).wait_recv()

        @pl.when(t < tiles - 1)
        def _():
            up(f).wait_recv()

        d = None
        for i in range(nh):
            near = db[i, f] + jnp.where(rows == 0, ht[f, i : i + 1, :], 0.0)
            near = near + jnp.where(rows == nrows - 1, hb[f, i : i + 1, :], 0.0)
            d_new = (hh[...] * near) * ip[i]
            d = d_new if d is None else d_new + gg[i] * d
            db[i, f] = d
        mid2(f).start()
        return carry

    def give(f):
        return remote(
            fb.at[pl.ds((1 - c) * half, half), f], out.at[:, c * nf + f],
            o_s.at[f], o_r.at[f], t, partner,
        )

    def keep(f):
        return pltpu.make_async_copy(
            fb.at[pl.ds(c * half, half), f], out.at[:, c * nf + f], ol.at[f]
        )

    def backward2(f, carry):
        mid2(f).wait()
        v = None
        for i in range(nh - 1, -1, -1):
            if v is None:
                v = (db[i, f] + cp[i] * mr2[f]) * den[...]
            else:
                v = db[i, f] + cp[i] * v
            fb[at(i), f] = fb[at(i), f] + v
        give(f).start()
        keep(f).start()
        return carry

    def folded(buffer, size):
        value = buffer[0]
        for k in range(1, size):
            value = value + buffer[k]
        return value

    for copy in stage1:
        copy.wait()
    s2[z] = folded(s1, 4 * ny)
    for copy in stage2:
        copy.start()

    lax.fori_loop(0, nf, forward2, 0)

    for copy in stage2:
        copy.wait()
    res[...] = folded(s2, nz) * scale
    for copy in gathers():
        copy.start()
    own_sum.start()

    lax.fori_loop(0, nf, backward2, 0)

    for d in range(4):
        for dc in range(2):
            if d or dc:
                place = slot((c + dc) % 2, (x - d + 4) % 4)
                remote(res, place, g_s.at[d, dc], g_r.at[d, dc], t, partner).wait_recv()
    own_sum.wait()

    for copy in spread + tags + [swap] + gathers():
        copy.wait_send()

    @pl.when(t > 0)
    def _():
        ghost_up.wait_send()

    @pl.when(t < tiles - 1)
    def _():
        ghost_down.wait_send()

    def drain(f, carry):
        @pl.when(t > 0)
        def _():
            up(f).wait_send()

        @pl.when(t < tiles - 1)
        def _():
            down(f).wait_send()

        keep(f).wait()
        give(f).wait()
        return carry

    lax.fori_loop(0, nf, drain, 0)


def shards(forcing, vert_coupling, horiz_coupling, basal_velocity, group_label, ice_mask):
    tiles = lax.axis_size("tile")
    layers, functionals, rows, width = forcing.shape
    nf = functionals // 2
    nh = 2 * layers
    nl = 4 * layers
    nz = min(8, tiles // 2)
    ny = tiles // (2 * nz)
    scale = -((tiles * rows * width / GROUPS) ** (-0.5))
    dma = pltpu.SemaphoreType.DMA
    vmem = pltpu.VMEM
    field = vmem((nh, nf, rows, width), F32)
    per_f = vmem((nf, rows, width), F32)
    per_layer = vmem((nh, rows, width), F32)
    flat = vmem((rows, width), F32)
    tile = vmem((rows, LANES), F32)
    whole = vmem((rows, LANES), jnp.int32)
    edge = vmem((nf, nh, width), F32)
    ghost = vmem((2 * nh + 1, width), F32)
    pieces = vmem((4, nf, LANES), F32)
    scratch = [
        tile, flat, tile, whole, whole,
        vmem((2, rows, LANES), F32), vmem((4, nl, rows, LANES), F32), vmem((4, 2, rows, LANES), F32),
        field, field, per_f, per_layer, per_layer, per_layer, per_layer,
        per_layer, per_layer, vmem((4, rows, width), F32), flat, vmem((2, nh, width), F32),
        flat, per_f, per_f,
        edge, edge, edge, edge, vmem((2, 2 * nh + 1, width), F32), ghost, ghost,
        vmem((rows + 2, nf, width), F32), vmem((rows + 2, LANES, width), jnp.bfloat16),
        pieces, vmem((4 * ny, nf, LANES), F32), vmem((nz, nf, LANES), F32),
        vmem((nf, LANES), F32),
        dma((7,)), dma((2,)), dma((3,)), dma((3,)), dma((3,)), dma((3,)),
        dma((nf,)), dma((nf,)), dma((nf,)), dma((nf,)),
        dma((nf,)), dma((nf,)), dma((nf,)), dma((nf,)),
        dma, dma, dma, dma,
        dma((nf,)), dma((nf,)), dma((nf,)),
        dma((2, 16)), dma((2, 16)), dma((4, 2)), dma((4, 2)), pltpu.SemaphoreType.REGULAR((3,)),
    ]
    operands = (forcing, vert_coupling, horiz_coupling, basal_velocity, group_label, ice_mask)
    return pl.pallas_call(
        functools.partial(kernel, tiles, scale),
        out_shape=(
            jax.ShapeDtypeStruct(forcing.shape, F32),
            jax.ShapeDtypeStruct((functionals, GROUPS), F32),
        ),
        in_specs=[pl.BlockSpec(memory_space=pltpu.HBM)] * 6,
        out_specs=(pl.BlockSpec(memory_space=pl.ANY), pl.BlockSpec(memory_space=pl.ANY)),
        scratch_shapes=scratch,
        compiler_params=pltpu.CompilerParams(
            collective_id=0, has_side_effects=True, vmem_limit_bytes=32 * 1024 * 1024
        ),
        name="sweeps",
    )(*[pltpu.with_memory_space_constraint(operand, pltpu.HBM) for operand in operands])


def solution(mesh):
    in_specs = (
        P("layer", None, "tile", None),
        P(None, "tile", "layer"),
        P("tile", None),
        P("tile", "layer"),
        P("tile", "layer"),
        P("tile", "layer"),
    )
    out_specs = (P("layer", None, "tile", None), P())
    return jax.shard_map(shards, mesh=mesh, in_specs=in_specs, out_specs=out_specs, check_vma=False)
```

```python
import functools

import jax
import jax.numpy as jnp
from jax import lax
from jax.experimental import pallas as pl
from jax.experimental.pallas import tpu as pltpu
from jax.sharding import PartitionSpec as P

GROUPS = 512
LANES = 128
MESH = pl.DeviceIdType.MESH
F32 = jnp.float32


def farthest_first(steps, sizes):
    def hops(step):
        return sum(min(k, size - k) for k, size in zip(step, sizes))

    return sorted((step for step in steps if hops(step)), key=hops, reverse=True)


def kernel(
    tiles, scale,
    forc, vert, horiz, basal, label, mask,
    out, sens,
    v0, hh, bb, ll, mm, pack, vb, wl, fb, db, va, ip, gg, cp, mw, cpo, mwo, gam, rw, er, den, mr, mr2,
    et, eb, ht, hb, gs, gt, gb, zz, oh, part, s1, s2, res,
    lsem, fsem, c_s, c_r, w_s, w_r, m1_s, m1_r, m2_s, m2_r,
    up_s, up_r, dn_s, dn_r, gu_s, gu_r, gd_s, gd_r, o_s, o_r, ol, r_s, r_r, g_s, g_r, hello,
):
    nf = fb.shape[1]
    nh = fb.shape[0]
    half = nh // 2
    nrows, width = hh.shape
    blocks = width // LANES
    nz = min(8, tiles // 2)
    ny = tiles // (2 * nz)
    t = lax.axis_index("tile")
    l = lax.axis_index("layer")
    p = l // 2
    c = l - 2 * p
    z = t % nz
    x = 2 * ((t // nz) % 2) + p
    y = t // (2 * nz)
    partner = 2 * p + 1 - c
    cross = 2 * (1 - p) + c
    diag = 2 * (1 - p) + 1 - c

    def at_x(number):
        return t + nz * (number // 2 - (x // 2)), 2 * (number % 2)

    def remote(src, dst, ssem, rsem, tile, layer):
        return pltpu.make_async_remote_copy(
            src_ref=src, dst_ref=dst, send_sem=ssem, recv_sem=rsem,
            device_id=(tile, layer), device_id_type=MESH,
        )

    barrier = pltpu.get_barrier_semaphore()
    first = jnp.logical_and(z == 0, t > 0)
    last = jnp.logical_and(z == nz - 1, t < tiles - 1)
    beside, side_layer = at_x((x + 3 + 2 * (x % 2)) % 4)
    near = [
        (t, cross), (t, diag), (t, partner), (beside, side_layer + c),
        (t - z + (z + 1) % nz, l), (t - z + (z + nz - 1) % nz, l),
    ]
    if ny > 1:
        near.append((t + 2 * nz * ((y + 1) % ny - y), l))
        near.append((t + 2 * nz * ((y + ny - 1) % ny - y), l))

    def tell_near(semaphore):
        for tile, layer in near:
            pl.semaphore_signal(
                semaphore, inc=1, device_id=(tile, layer), device_id_type=MESH
            )

    tell_near(barrier)

    local = [
        pltpu.make_async_copy(vert.at[0], v0, lsem.at[0]),
        pltpu.make_async_copy(horiz, hh, lsem.at[1]),
        pltpu.make_async_copy(basal, bb, lsem.at[2]),
        pltpu.make_async_copy(label, ll, lsem.at[3]),
        pltpu.make_async_copy(mask, mm, lsem.at[4]),
    ]
    for copy in local:
        copy.start()
    own = pltpu.make_async_copy(vert, vb.at[l], lsem.at[5])
    own.start()
    stay = pltpu.make_async_copy(
        forc.at[:, pl.ds(c * nf, nf)], fb.at[pl.ds(c * half, half)], lsem.at[6]
    )
    stay.start()

    pl.semaphore_wait(barrier, len(near))

    spread = [
        remote(vert, vb.at[l], c_s.at[k], c_r.at[k], t, layer)
        for k, layer in enumerate((cross, diag, partner))
    ]
    for copy in spread:
        copy.start()
    tell_near(hello.at[0])
    swap = remote(
        forc.at[:, pl.ds((1 - c) * nf, nf)], fb.at[pl.ds(c * half, half)],
        fsem.at[0], fsem.at[1], t, partner,
    )

    for copy in local:
        copy.wait()
    pack[0] = v0[...] * bb[...] * mm[...].astype(F32)
    pack[1] = ll[...].astype(F32)
    tags = [
        remote(pack, wl.at[l], w_s.at[k], w_r.at[k], t, layer)
        for k, layer in enumerate((cross, diag, partner))
    ]
    for copy in tags:
        copy.start()
    swap.start()

    for k in range(2):
        pl.semaphore_wait(hello.at[k], len(near))
        tell_near(hello.at[k + 1])
    wl[l] = pack[...]

    @pl.when(t == 0)
    def _():
        ht[...] = jnp.zeros_like(ht)
        gt[...] = jnp.zeros_like(gt)

    @pl.when(t == tiles - 1)
    def _():
        hb[...] = jnp.zeros_like(hb)
        gb[...] = jnp.zeros_like(gb)

    own.wait()
    for copy in spread:
        copy.wait_recv()

    h4 = 4.0 * hh[...]

    def coupling(i, chip):
        value = jnp.concatenate(
            [vb[q, (i if i else 15 * chip) + chip * (16 - 2 * i if i else 0)] for q in range(blocks)],
            axis=1,
        )
        return value if i else value * (1 - chip).astype(F32)

    def pivots(chip):
        outer = coupling(0, chip)
        prev = None
        for i in range(nh):
            inner = coupling(i + 1, chip)
            pivot = outer + inner + h4
            if prev is not None:
                pivot = pivot - outer * prev
            inverse = 1.0 / pivot
            prev = inner * inverse
            yield inverse, outer * inverse, prev
            outer = inner

    lower = (1 - p).astype(F32)
    for i, (inverse, scaled, ahead) in enumerate(pivots(p)):
        ip[i] = inverse
        gg[i] = scaled
        cp[i] = ahead

    def at(i):
        return i + p * (nh - 1 - 2 * i)

    def mid1(f):
        return remote(fb.at[at(nh - 1), f], mr.at[f], m1_s.at[f], m1_r.at[f], t, cross)

    def mid2(f):
        return remote(db.at[nh - 1, f], mr2.at[f], m2_s.at[f], m2_r.at[f], t, cross)

    def up(f):
        return remote(et.at[f], hb.at[f], up_s.at[f], up_r.at[f], t - 1, l)

    def down(f):
        return remote(eb.at[f], ht.at[f], dn_s.at[f], dn_r.at[f], t + 1, l)

    ghost_up = remote(gs.at[0], gb, gu_s, gu_r, t - 1, l)
    ghost_down = remote(gs.at[1], gt, gd_s, gd_r, t + 1, l)

    def forward1(f, carry):
        d = None
        for i in range(nh):
            d_new = fb[at(i), f] * ip[i]
            d = d_new if d is None else d_new + gg[i] * d
            fb[at(i), f] = d
        mid1(f).start()
        return carry


    def mark(r, row):
        low = row.astype(jnp.int32) % LANES
        groups = lax.broadcasted_iota(jnp.int32, (LANES, width), 0)
        oh[r] = (groups == low).astype(F32).astype(jnp.bfloat16)

    def label_row(r):
        return jnp.concatenate([wl[q, 1, r : r + 1, :] for q in range(blocks)], axis=1)

    for copy in tags:
        copy.wait_recv()
    weight = jnp.concatenate([wl[q, 0] for q in range(blocks)], axis=1)
    factor = weight * hh[...]
    upper = 1.0 - lower
    for i, (inverse, scaled, ahead) in enumerate(pivots(1 - p)):
        far = inverse * upper if i == 0 else scaled * far
        mwo[i] = far
        cpo[i] = ahead
    unit = None
    for i in range(nh):
        unit = ip[i] * lower if unit is None else gg[i] * unit
        mw[i] = unit
    middle = cp[nh - 1]
    inverse = 1.0 / (1.0 - middle * ahead)
    den[...] = inverse
    m = (unit + middle * far) * inverse
    mo = (far + ahead * unit) * inverse
    shape = (nrows, width)
    rows = lax.broadcasted_iota(jnp.int32, shape, 0)
    columns = lax.broadcasted_iota(jnp.int32, shape, 1)

    def neighbours(v):
        return (
            jnp.where(rows == 0, 0.0, pltpu.roll(v, 1, axis=0)),
            jnp.where(rows == nrows - 1, 0.0, pltpu.roll(v, nrows - 1, axis=0)),
            jnp.where(columns == 0, 0.0, pltpu.roll(v, 1, axis=1)),
            jnp.where(columns == width - 1, 0.0, pltpu.roll(v, width - 1, axis=1)),
        )

    for i in range(nh - 1, -1, -1):
        if i < nh - 1:
            m = mw[i] + cp[i] * m
            mo = mwo[i] + cpo[i] * mo
        mi = m * factor
        moi = mo * factor
        mw[i] = mi
        for side, row in ((0, 0), (1, nrows - 1)):
            gs[side, i : i + 1, :] = mi[row : row + 1, :]
            gs[side, nh + i : nh + i + 1, :] = moi[row : row + 1, :]
        mwo[i] = moi
    gs[0, 2 * nh : 2 * nh + 1, :] = label_row(0)
    gs[1, 2 * nh : 2 * nh + 1, :] = label_row(nrows - 1)

    pl.semaphore_wait(hello.at[2], len(near))

    @pl.when(last)
    def _():
        ghost_down.start()

    @pl.when(t > 0)
    def _():
        ghost_up.start()

    @pl.when(z < nz - 1)
    def _():
        ghost_down.start()

    reach = None
    across = None
    for i in range(nh - 1, -1, -1):
        reach = cpo[i] if reach is None else cpo[i] * reach
        for side, row in ((0, 0), (1, nrows - 1)):
            er[side, i : i + 1, :] = reach[row : row + 1, :]
        terms = [mwo[i] * v for v in neighbours(reach)]
        across = terms if across is None else [v + w for v, w in zip(across, terms)]
    for k in range(4):
        gam[k] = across[k]
    rw[...] = reach * (weight * upper)

    stay.wait()
    swap.wait_recv()
    lax.fori_loop(0, nf, forward1, 0)

    for r in range(nrows):
        mark(r, label_row(r))

    def bed(f, carry):
        v = None
        total = None
        for i in range(nh - 1, -1, -1):
            if v is None:
                v = fb[at(i), f] * den[...]
                parts = neighbours(v)
                total = rw[...] * v
                for k in range(4):
                    total = total + gam[k] * parts[k]
            else:
                v = fb[at(i), f] + cp[i] * v
                parts = neighbours(v)
            total = total + mw[i] * ((parts[0] + parts[1]) + (parts[2] + parts[3]))
            et[f, i : i + 1, :] = v[0:1, :]
            eb[f, i : i + 1, :] = v[nrows - 1 : nrows, :]
        va[f] = total + (weight * lower) * v
        return carry

    lax.fori_loop(0, nf, bed, 0)

    for f in range(nf):
        v = va[f]
        for r in range(nrows):
            zz[r, f : f + 1, :] = v[r : r + 1, :]

    @pl.when(t > 0)
    def _():
        ghost_down.wait_recv()

    @pl.when(t < tiles - 1)
    def _():
        ghost_up.wait_recv()

    mark(nrows, gt[2 * nh : 2 * nh + 1, :])
    mark(nrows + 1, gb[2 * nh : 2 * nh + 1, :])
    beyond_up = jnp.sum(gt[nh : 2 * nh, :] * er[0], axis=0, keepdims=True)
    beyond_down = jnp.sum(gb[nh : 2 * nh, :] * er[1], axis=0, keepdims=True)
    for f in range(nf):
        first_row = jnp.sum(gt[0:nh, :] * et[f], axis=0, keepdims=True)
        last_row = jnp.sum(gb[0:nh, :] * eb[f], axis=0, keepdims=True)
        zz[nrows, f : f + 1, :] = first_row + beyond_up * et[f, nh - 1 : nh, :]
        zz[nrows + 1, f : f + 1, :] = last_row + beyond_down * eb[f, nh - 1 : nh, :]
    total = jnp.zeros((12 * nf, LANES), F32)
    for r in range(nrows + 2):
        if r < nrows:
            row = label_row(r)
        else:
            row = (gt if r == nrows else gb)[2 * nh : 2 * nh + 1, :]
        high = row.astype(jnp.int32) // LANES
        v = zz[r]
        apart = jnp.concatenate([jnp.where(high == g, v, 0.0) for g in range(4)], axis=0)
        a0 = apart.astype(jnp.bfloat16)
        rest = apart - a0.astype(F32)
        a1 = rest.astype(jnp.bfloat16)
        a2 = (rest - a1.astype(F32)).astype(jnp.bfloat16)
        total += lax.dot_general(
            jnp.concatenate([a0, a1, a2], axis=0), oh[r],
            (((1,), (1,)), ((), ())), preferred_element_type=F32,
        )
    n = 4 * nf
    sums = (total[2 * n :] + total[n : 2 * n]) + total[:n]
    for g in range(4):
        part[g] = sums[g * nf : (g + 1) * nf]

    place = 4 * y + x
    s1[place] = part[x]
    stage1 = []
    for e, d in farthest_first([(e, d) for e in range(ny) for d in range(4)], (ny, 4)):
        there = (x + d) % 4
        tile, layer = at_x(there)
        tile = tile + 2 * nz * ((y + e) % ny - y)
        stage1.append(
            remote(part.at[there], s1.at[place], r_s.at[0, 4 * e + d],
                   r_r.at[0, 4 * e + d], tile, layer + c)
        )
    for copy in stage1:
        copy.start()

    def backward1(f, carry):
        mid1(f).wait()
        v = None
        for i in range(nh - 1, -1, -1):
            if v is None:
                v = (fb[at(i), f] + cp[i] * mr[f]) * den[...]
            else:
                v = fb[at(i), f] + cp[i] * v
            fb[at(i), f] = v
            et[f, i : i + 1, :] = v[0:1, :]
            eb[f, i : i + 1, :] = v[nrows - 1 : nrows, :]
            parts = neighbours(v)
            db[i, f] = (parts[0] + parts[1]) + (parts[2] + parts[3])

        @pl.when(z > 0)
        def _():
            up(f).start()

        @pl.when(z < nz - 1)
        def _():
            down(f).start()

        return carry

    lax.fori_loop(0, nf, backward1, 0)

    @pl.when(first)
    def _():
        lax.fori_loop(0, nf, lambda f, k: (up(f).start(), k)[1], 0)

    @pl.when(last)
    def _():
        lax.fori_loop(0, nf, lambda f, k: (down(f).start(), k)[1], 0)

    def exchange(number, buffer, size, mine, stride):
        return [
            remote(buffer.at[mine], buffer.at[mine], r_s.at[number, d - 1], r_r.at[number, d - 1],
                   t + stride * ((mine + d) % size - mine), l)
            for (d,) in farthest_first([(d,) for d in range(size)], (size,))
        ]

    stage2 = exchange(1, s2, nz, z, 1)

    def slot(core, number):
        return sens.at[
            pl.ds(pl.multiple_of(core * nf, nf), nf),
            pl.ds(pl.multiple_of(number * LANES, LANES), LANES),
        ]

    own_sum = pltpu.make_async_copy(res, slot(c, x), lsem.at[4])

    def gathers():
        copies = []
        for d, dc in farthest_first([(d, dc) for d in range(4) for dc in range(2)], (4, 2)):
            tile, layer = at_x((x + d) % 4)
            copies.append(
                remote(res, slot(c, x), g_s.at[d, dc], g_r.at[d, dc],
                       tile, layer + (c + dc) % 2)
            )
        return copies

    def forward2(f, carry):
        @pl.when(t > 0)
        def _():
            down(f).wait_recv()

        @pl.when(t < tiles - 1)
        def _():
            up(f).wait_recv()

        d = None
        for i in range(nh):
            near = db[i, f] + jnp.where(rows == 0, ht[f, i : i + 1, :], 0.0)
            near = near + jnp.where(rows == nrows - 1, hb[f, i : i + 1, :], 0.0)
            d_new = (hh[...] * near) * ip[i]
            d = d_new if d is None else d_new + gg[i] * d
            db[i, f] = d
        mid2(f).start()
        return carry

    def give(f):
        return remote(
            fb.at[pl.ds((1 - c) * half, half), f], out.at[:, c * nf + f],
            o_s.at[f], o_r.at[f], t, partner,
        )

    def keep(f):
        return pltpu.make_async_copy(
            fb.at[pl.ds(c * half, half), f], out.at[:, c * nf + f], ol.at[f]
        )

    def backward2(f, carry):
        mid2(f).wait()
        v = None
        for i in range(nh - 1, -1, -1):
            if v is None:
                v = (db[i, f] + cp[i] * mr2[f]) * den[...]
            else:
                v = db[i, f] + cp[i] * v
            fb[at(i), f] = fb[at(i), f] + v
        give(f).start()
        keep(f).start()
        return carry

    def folded(buffer, size):
        value = buffer[0]
        for k in range(1, size):
            value = value + buffer[k]
        return value

    for copy in stage1:
        copy.wait()
    s2[z] = folded(s1, 4 * ny)
    for copy in stage2:
        copy.start()

    lax.fori_loop(0, nf, forward2, 0)

    for copy in stage2:
        copy.wait()
    res[...] = folded(s2, nz) * scale
    for copy in gathers():
        copy.start()
    own_sum.start()

    lax.fori_loop(0, nf, backward2, 0)

    for d in range(4):
        for dc in range(2):
            if d or dc:
                place = slot((c + dc) % 2, (x - d + 4) % 4)
                remote(res, place, g_s.at[d, dc], g_r.at[d, dc], t, partner).wait_recv()
    own_sum.wait()

    for copy in spread + tags + [swap] + gathers():
        copy.wait_send()

    @pl.when(t > 0)
    def _():
        ghost_up.wait_send()

    @pl.when(t < tiles - 1)
    def _():
        ghost_down.wait_send()

    def drain(f, carry):
        @pl.when(t > 0)
        def _():
            up(f).wait_send()

        @pl.when(t < tiles - 1)
        def _():
            down(f).wait_send()

        keep(f).wait()
        give(f).wait()
        return carry

    lax.fori_loop(0, nf, drain, 0)


def shards(forcing, vert_coupling, horiz_coupling, basal_velocity, group_label, ice_mask):
    tiles = lax.axis_size("tile")
    layers, functionals, rows, width = forcing.shape
    nf = functionals // 2
    nh = 2 * layers
    nl = 4 * layers
    nz = min(8, tiles // 2)
    ny = tiles // (2 * nz)
    scale = -((tiles * rows * width / GROUPS) ** (-0.5))
    dma = pltpu.SemaphoreType.DMA
    vmem = pltpu.VMEM
    field = vmem((nh, nf, rows, width), F32)
    per_f = vmem((nf, rows, width), F32)
    per_layer = vmem((nh, rows, width), F32)
    flat = vmem((rows, width), F32)
    tile = vmem((rows, LANES), F32)
    whole = vmem((rows, LANES), jnp.int32)
    edge = vmem((nf, nh, width), F32)
    ghost = vmem((2 * nh + 1, width), F32)
    pieces = vmem((4, nf, LANES), F32)
    scratch = [
        tile, flat, tile, whole, whole,
        vmem((2, rows, LANES), F32), vmem((4, nl, rows, LANES), F32), vmem((4, 2, rows, LANES), F32),
        field, field, per_f, per_layer, per_layer, per_layer, per_layer,
        per_layer, per_layer, vmem((4, rows, width), F32), flat, vmem((2, nh, width), F32),
        flat, per_f, per_f,
        edge, edge, edge, edge, vmem((2, 2 * nh + 1, width), F32), ghost, ghost,
        vmem((rows + 2, nf, width), F32), vmem((rows + 2, LANES, width), jnp.bfloat16),
        pieces, vmem((4 * ny, nf, LANES), F32), vmem((nz, nf, LANES), F32),
        vmem((nf, LANES), F32),
        dma((7,)), dma((2,)), dma((3,)), dma((3,)), dma((3,)), dma((3,)),
        dma((nf,)), dma((nf,)), dma((nf,)), dma((nf,)),
        dma((nf,)), dma((nf,)), dma((nf,)), dma((nf,)),
        dma, dma, dma, dma,
        dma((nf,)), dma((nf,)), dma((nf,)),
        dma((2, 16)), dma((2, 16)), dma((4, 2)), dma((4, 2)), pltpu.SemaphoreType.REGULAR((3,)),
    ]
    operands = (forcing, vert_coupling, horiz_coupling, basal_velocity, group_label, ice_mask)
    return pl.pallas_call(
        functools.partial(kernel, tiles, scale),
        out_shape=(
            jax.ShapeDtypeStruct(forcing.shape, F32),
            jax.ShapeDtypeStruct((functionals, GROUPS), F32),
        ),
        in_specs=[pl.BlockSpec(memory_space=pltpu.HBM)] * 6,
        out_specs=(pl.BlockSpec(memory_space=pl.ANY), pl.BlockSpec(memory_space=pl.ANY)),
        scratch_shapes=scratch,
        compiler_params=pltpu.CompilerParams(
            collective_id=0, has_side_effects=True, vmem_limit_bytes=32 * 1024 * 1024
        ),
        name="sweeps",
    )(*[pltpu.with_memory_space_constraint(operand, pltpu.HBM) for operand in operands])


def solution(mesh):
    in_specs = (
        P("layer", None, "tile", None),
        P(None, "tile", "layer"),
        P("tile", None),
        P("tile", "layer"),
        P("tile", "layer"),
        P("tile", "layer"),
    )
    out_specs = (P("layer", None, "tile", None), P())
    return jax.shard_map(shards, mesh=mesh, in_specs=in_specs, out_specs=out_specs, check_vma=False)
```
